256 devices in a mesh: grid: 16 (over z, y_lo), chan: 16 (over x, y_hi, core).
Axes of the slice: x: 4, y: 4 (y_hi: 2, y_lo: 2; y = y_hi * 2 + y_lo), z: 8, core: 2. Of those that a mesh axis runs over, the one named last changes fastest.
Arguments:
- spectra: bfloat16 [2, 8, 48, 4096], P(None, None, 'grid', 'chan'), may hold values from -90 to 90, as said below
- travel: int32 [65536, 4096], P('grid', 'chan'), may hold values from 0 to 2047
- quality: int32 [4096], P('chan'), may hold values 0 or 1
Outputs:
- beam_power: float32 [48, 65536], P(None, ('grid', 'chan'))
The draws below stay inside these ranges and needn't reach their ends.
Inputs may be any that keep to these rules, and one draw needn't show every extreme that they name: `spectra`: spectra of the windows; scales differ between channels and between windows.
All inputs are finite; a program needn't handle non-finite values. No bound on the sum of `quality` on one device may be relied on, other than what follows from the above.
Results may differ from the reference program's by a relative error of at most 0.0012.
Values may be sent and summed in bfloat16 or wider, within the bound.
No kernel may reach another device: no remote copies, remote signals or barrier semaphores. Data moves between devices by JAX's collectives and lax.ppermute only.
A program may use at most 64 MiB of HBM per device.

```python
import math
import jax
import jax.numpy as jnp
from jax import lax

C = 4096
F = 8
NFFT = 2048
W = 48
G = 65536
N_CHAN = 16


def draw_spectra(key, part):
    subkeys = jax.random.split(key, 3)
    positions = jnp.arange(C, dtype=jnp.float32) / C
    rising = jnp.exp(positions * math.log(3.0))
    roughness = jnp.exp(jax.random.uniform(subkeys[1], (C,), jnp.float32, 0.0, math.log(10.0)))
    window_scale = jnp.exp(jax.random.uniform(subkeys[2], (W,), jnp.float32, math.log(0.3), math.log(3.0)))
    scales = 0.3 * window_scale[:, None] * (rising * roughness)[None, :]
    noise_part = jnp.clip(jax.random.normal(subkeys[0], (2, F, W, C), jnp.float32), -3.0, 3.0)
    drawn_values = noise_part * scales
    return drawn_values.astype(jnp.bfloat16)


def touch_ends(values, stream_key, smallest, largest):
    extent = values.shape
    spot = [jax.random.randint(jax.random.fold_in(stream_key, axis), (), 0, extent[axis]) for axis in range(len(extent))]
    values = values.at[tuple(spot)].set(smallest)
    longest = extent.index(max(extent))
    spot[longest] = (spot[longest] + 1) % extent[longest]
    return values.at[tuple(spot)].set(largest)


def setup_inputs(seed: int = 0) -> dict:
    key_of = jax.random.split(jax.random.key(seed), 4)
    return {
        "spectra": draw_spectra(jax.random.fold_in(key_of[3], 71), 0),
        "travel": touch_ends(jax.random.randint(key_of[1], (G, C), 0, 2048), jax.random.fold_in(key_of[1], 1), 0, 2047).astype(jnp.int32),
        "quality": touch_ends((jax.random.randint(key_of[2], (C,), 0, 8) < 7).astype(jnp.int32), jax.random.fold_in(key_of[2], 1), 0, 1),
    }


lowest_bin = 37
bin_spacing = 29


def replica_rows(delay_rows):
    freq_bins = lowest_bin + bin_spacing * jnp.arange(F, dtype=jnp.int32)
    phase_index = (freq_bins[:, None, None] * delay_rows[None, :, :]) % NFFT
    angles = phase_index.astype(jnp.float32) * (2.0 * math.pi / NFFT)
    return jnp.concatenate([jnp.cos(angles), jnp.sin(angles)], axis=2).astype(jnp.bfloat16)


def stacked_spectra(masked):
    real_part = masked[0]
    imag_part = masked[1]
    upper_half = jnp.concatenate([real_part, imag_part], axis=1)
    lower_half = jnp.concatenate([-imag_part, real_part], axis=1)
    return jnp.concatenate([upper_half, lower_half], axis=2)


def reference(spectra, travel, quality):
    masked = spectra * quality.astype(jnp.bfloat16)
    squared = masked.astype(jnp.float32) ** 2
    window_norm = jnp.sum(squared, axis=(0, 1, 3)) / (F * C) + 1e-6
    chan_width = C // N_CHAN
    row_count = math.gcd(G, 4096)

    def per_block(running, block_index):
        first_col = block_index * chan_width
        delay_table = lax.dynamic_slice_in_dim(travel, first_col, chan_width, 1)
        spectra_part = lax.dynamic_slice_in_dim(masked, first_col, chan_width, 3)
        spectra_matrix = stacked_spectra(spectra_part).astype(jnp.float32)

        def one_block(delay_rows):
            replicas = replica_rows(delay_rows).astype(jnp.float32)
            beam_terms = jnp.einsum("frk,fwk->rfw", replicas, spectra_matrix)
            return beam_terms.reshape(delay_rows.shape[0], -1)

        block_terms = lax.map(one_block, delay_table.reshape(G // row_count, row_count, chan_width))
        partial_beams = block_terms.reshape(G, -1)
        return running + partial_beams, None

    start_sum = jnp.zeros((G, 2 * F * W), jnp.float32)
    beams, unused = lax.scan(per_block, start_sum, jnp.arange(N_CHAN, dtype=jnp.int32))
    energies = jnp.sum(beams.reshape(G, 2 * F, W) ** 2, axis=1)
    beam_power = energies / (F * C * window_norm[None, :])
    return beam_power.T
```

```python
import functools

import jax
import jax.numpy as jnp
import numpy as np
from jax import lax
from jax.experimental import pallas as pl
from jax.experimental.pallas import tpu as pltpu
from jax.sharding import Mesh, PartitionSpec as P

NFFT = 2048
lowest_bin = 37
bin_spacing = 29
f32 = jnp.float32
bf16 = jnp.bfloat16

NF = 8
ROWS = 256
CH = 256
PIECES = 4
COLS = 96
FSTEP = 4
TILE = 16


def series_coefficients():
    nodes = np.cos(np.linspace(0, np.pi, 4002)) / 8
    squares = nodes**2
    angles = 2 * np.pi * nodes
    sine = np.linalg.lstsq(squares[:, None] ** np.arange(4), np.sin(angles) / nodes, rcond=None)[0]
    cosine = np.linalg.lstsq(squares[:, None] ** np.arange(5), np.cos(angles), rcond=None)[0]
    return [np.float32(v) for v in sine], [np.float32(v) for v in cosine]


SINE, COSINE = series_coefficients()


def horner(coefficients, value):
    total = coefficients[-1]
    for coefficient in coefficients[-2::-1]:
        total = coefficient + value * total
    return total


def unit_circle(turns_times, multiple):
    turns = turns_times * np.float32(multiple / NFFT)
    magic = np.float32(1.5 * 2**23)
    part = turns - ((turns + magic) - magic)
    quarter = part * np.float32(0.25)
    square = quarter * quarter
    sine = quarter * horner(SINE, square)
    cosine = horner(COSINE, square)
    for _ in range(2):
        twice = sine + sine
        sine, cosine = twice * cosine, np.float32(1.0) - twice * sine
    return cosine, sine


def replica_tiles(tau):
    delay = tau.astype(f32)
    c0, s0 = unit_circle(delay, lowest_bin)
    cd, sd = unit_circle(delay, bin_spacing)
    cosines = [c0, c0 * cd - s0 * sd]
    sines = [s0, s0 * cd + c0 * sd]
    twice = cd + cd
    for _ in range(2, NF):
        cosines.append(twice * cosines[-1] - cosines[-2])
        sines.append(twice * sines[-1] - sines[-2])
    return cosines, sines


def beams_kernel(place, t0, t1, t2, t3, w_ref, norm_ref, out_ref, rep_a, rep_b, total, *, with_norm):
    pieces = [t0, t1, t2, t3]
    reps = [rep_a, rep_b]
    steps = NF // FSTEP
    chunk = ROWS // steps

    def fill(piece, step, rep):
        for half in range(CH // 128):
            for tile in range(chunk // TILE):
                rows = pl.ds(pl.multiple_of(step * chunk + tile * TILE, TILE), TILE)
                tau = pieces[piece][0, rows, half * 128 : (half + 1) * 128].astype(jnp.int32)
                cosines, sines = replica_tiles(tau)
                for f in range(NF):
                    rep[f, rows, half * 128 : (half + 1) * 128] = cosines[f].astype(bf16)
                    rep[f, rows, CH + half * 128 : CH + (half + 1) * 128] = sines[f].astype(bf16)

    def multiply(piece, step, rep):
        for q in range(FSTEP):
            f = step * FSTEP + q
            part = lax.dot_general(
                rep[f], w_ref[f, piece], (((1,), (1,)), ((), ())), preferred_element_type=f32
            )
            total[f] = part if piece == 0 else total[f] + part

    def loop(body):
        lax.fori_loop(0, steps, lambda step, carry: (body(step), carry)[1], 0)

    loop(lambda step: fill(0, step, reps[0]))
    for piece in range(PIECES):
        def body(step, piece=piece):
            multiply(piece, step, reps[piece % 2])
            if piece < PIECES - 1:
                fill(piece + 1, step, reps[(piece + 1) % 2])
        loop(body)
    for part in range(ROWS // 128):
        rows = slice(part * 128, (part + 1) * 128)
        joined = jnp.concatenate([total[f, rows] for f in range(NF)], axis=1)
        out_ref[rows] = joined.astype(out_ref.dtype)
    if with_norm:
        out_ref[ROWS : ROWS + 16] = norm_ref[...]


def beams_block(place, pieces, weights, norm_rows, shift, out_dtype):
    with_norm = shift != 0
    out_rows = ROWS + 16 if with_norm else ROWS
    piece = pl.BlockSpec((1, ROWS, CH), lambda i, p: ((p[0] + shift) % 4, 0, 0))
    vmem = pl.BlockSpec(memory_space=pltpu.VMEM)
    return pl.pallas_call(
        functools.partial(beams_kernel, with_norm=with_norm),
        grid_spec=pltpu.PrefetchScalarGridSpec(
            num_scalar_prefetch=1,
            grid=(1,),
            in_specs=[piece, piece, piece, piece, vmem, pl.BlockSpec((16, NF * COLS), lambda i, p: (0, 0))],
            out_specs=pl.BlockSpec((out_rows, NF * COLS), lambda i, p: (0, 0)),
            scratch_shapes=[
                pltpu.VMEM((NF, ROWS, 2 * CH), bf16),
                pltpu.VMEM((NF, ROWS, 2 * CH), bf16),
                pltpu.VMEM((NF, ROWS, COLS), f32),
            ],
        ),
        out_shape=jax.ShapeDtypeStruct((out_rows, NF * COLS), out_dtype),
        cost_estimate=pl.CostEstimate(flops=6_000_000_000, bytes_accessed=4_000_000, transcendentals=0),
        compiler_params=pltpu.CompilerParams(vmem_limit_bytes=24 << 20),
        name=f"beams_{shift}",
    )(place, *pieces, weights, norm_rows)


def prepare_kernel(place, own_ref, other_ref, w_ref, norm_ref, wide):
    squares = jnp.zeros((COLS, CH), f32)
    for piece in range(PIECES):
        source = own_ref if piece % 2 == 0 else other_ref
        block = place[1] ^ (piece // 2)
        for g in range(16):
            for half in range(CH // 128):
                lanes = slice(half * 128, (half + 1) * 128)
                wide[half, g * 48 : (g + 1) * 48, :] = source[g, block, :, lanes].astype(f32)
        for f in range(NF):
            parts = [
                [
                    jnp.concatenate(
                        [
                            wide[half, pl.ds(p * 24 + f * 3 + i, 16, stride=48), :]
                            for half in range(CH // 128)
                        ],
                        axis=1,
                    )
                    for i in range(3)
                ]
                for p in range(2)
            ]
            real = jnp.concatenate(parts[0], axis=0)
            imag = jnp.concatenate(parts[1], axis=0)
            both = jnp.concatenate([real, imag], axis=0)
            squares = squares + both * both
            w_ref[f, piece, :, 0:CH] = both.astype(bf16)
            w_ref[f, piece, :, CH : 2 * CH] = jnp.concatenate([-imag, real], axis=0).astype(bf16)
    sums = lax.dot_general(
        jnp.ones((16, CH), f32), squares, (((1,), (1,)), ((), ())),
        preferred_element_type=f32, precision=lax.Precision.HIGHEST,
    )
    high = sums.astype(bf16).astype(f32)
    middle = (sums - high).astype(bf16).astype(f32)
    low = sums - high - middle
    row = lax.broadcasted_iota(jnp.int32, sums.shape, 0)
    zero = jnp.zeros_like(sums)
    split = jnp.where(row == 0, high, jnp.where(row == 1, middle, jnp.where(row == 2, low, zero)))
    norm_ref[...] = jnp.concatenate([split] + [zero] * (NF - 1), axis=1).astype(bf16)


def prepare(place, own, other):
    whole = pl.BlockSpec(own.shape, lambda i, p: (0, 0, 0, 0))
    return pl.pallas_call(
        prepare_kernel,
        grid_spec=pltpu.PrefetchScalarGridSpec(
            num_scalar_prefetch=1,
            grid=(1,),
            in_specs=[whole, whole],
            out_specs=[
                pl.BlockSpec(memory_space=pltpu.VMEM),
                pl.BlockSpec((16, NF * COLS), lambda i, p: (0, 0)),
            ],
            scratch_shapes=[pltpu.VMEM((CH // 128, 768, 128), f32)],
        ),
        out_shape=[
            jax.ShapeDtypeStruct((NF, PIECES, COLS, 2 * CH), bf16),
            jax.ShapeDtypeStruct((16, NF * COLS), bf16),
        ],
        compiler_params=pltpu.CompilerParams(vmem_limit_bytes=24 << 20),
        name="prepare",
    )(place, own, other)


def selection():
    column = np.arange(NF * COLS)
    slot = column % 48
    window = 3 * (slot % 16) + slot // 16
    return (np.arange(48)[:, None] == window[None, :]).astype(np.float32)


def finish_kernel(r1, r2, r3, own_ref, norm_ref, pick_ref, out_ref, *, count):
    def total_of(rows):
        return r1[rows].astype(f32) + r2[rows].astype(f32) + r3[rows].astype(f32)

    def pick(values):
        return lax.dot_general(
            pick_ref[...], values, (((1,), (1,)), ((), ())),
            preferred_element_type=f32, precision=lax.Precision.HIGHEST,
        )

    beams = own_ref[...] + total_of(slice(0, ROWS))
    norm_rows = norm_ref[...].astype(f32) + total_of(slice(ROWS, ROWS + 16))
    norm_sum = jnp.sum(pick(norm_rows), axis=1, keepdims=True)
    window_norm = norm_sum / count + 1e-06
    out_ref[...] = pick(beams * beams) / (count * window_norm)


def finish(received, own, norm_rows, count):
    pick = jnp.asarray(selection())
    return pl.pallas_call(
        functools.partial(finish_kernel, count=count),
        out_shape=jax.ShapeDtypeStruct((48, ROWS), f32),
        compiler_params=pltpu.CompilerParams(vmem_limit_bytes=24 << 20),
        name="finish",
    )(*received, own, norm_rows, pick)


def per_device(spectra, travel, quality):
    masked = (spectra * quality.astype(bf16)).reshape(48, CH)
    place = jnp.stack([lax.axis_index("x"), lax.axis_index("yh"), lax.axis_index("c")]).astype(jnp.int32)
    yh, core = place[1], place[2]
    blocks = travel.reshape(4, 2, 2, ROWS, CH)

    def travel_for(flip_y, flip_c):
        return lax.dynamic_slice(
            blocks, (0, yh ^ flip_y, core ^ flip_c, 0, 0), (4, 1, 1, ROWS, CH)
        ).reshape(4, ROWS, CH).astype(jnp.int16)

    parts = [travel_for(flip // 2, flip % 2) for flip in range(4)]
    copies = jnp.broadcast_to(masked[None], (32, 48, CH))
    copies, *parts = lax.optimization_barrier((copies, *parts))
    pieces = parts[:1] + [
        lax.ppermute(parts[flip], ("yh", "c"), [(i, i ^ flip) for i in range(4)])
        for flip in (1, 2, 3)
    ]
    own = lax.all_to_all(copies, ("z", "yl", "yh"), 0, 0, tiled=True).reshape(16, 2, 48, CH)
    own, pieces[2], pieces[3] = lax.optimization_barrier((own, pieces[2], pieces[3]))
    other = lax.ppermute(own, "c", [(0, 1), (1, 0)])
    weights, norm_rows = prepare(place, own, other)
    received = []
    for shift in (2, 1, 3):
        beams = beams_block(place, pieces, weights, norm_rows, shift, bf16)
        received.append(lax.ppermute(beams, "x", [(i, (i + shift) % 4) for i in range(4)]))
    mine = beams_block(place, pieces, weights, norm_rows, 0, f32)
    return finish(received, mine, norm_rows, float(NF * CH * 16))


def solution(mesh):
    fine = Mesh(mesh.devices.reshape(8, 2, 4, 2, 2), ("z", "yl", "x", "yh", "c"))
    return jax.shard_map(
        per_device,
        mesh=fine,
        in_specs=(
            P(None, None, ("z", "yl"), ("x", "yh", "c")),
            P(("z", "yl"), ("x", "yh", "c")),
            P(("x", "yh", "c")),
        ),
        out_specs=P(None, ("z", "yl", "x", "yh", "c")),
        check_vma=False,
    )
```

```python
import functools

import jax
import jax.numpy as jnp
import numpy as np
from jax import lax
from jax.experimental import pallas as pl
from jax.experimental.pallas import tpu as pltpu
from jax.sharding import Mesh, PartitionSpec as P

NFFT = 2048
lowest_bin = 37
bin_spacing = 29
f32 = jnp.float32
bf16 = jnp.bfloat16

NF = 8
ROWS = 256
CH = 256
COLS = 96
TILE = 32
NORM_ROWS = 8


def series_coefficients():
    nodes = np.cos(np.linspace(0, np.pi, 4002)) / 8
    squares = nodes**2
    angles = 2 * np.pi * nodes
    sine = np.linalg.lstsq(squares[:, None] ** np.arange(4), np.sin(angles) / nodes, rcond=None)[0]
    cosine = np.linalg.lstsq(squares[:, None] ** np.arange(5), np.cos(angles), rcond=None)[0]
    return [np.float32(v) for v in sine], [np.float32(v) for v in cosine]


SINE, COSINE = series_coefficients()


def horner(coefficients, value):
    total = coefficients[-1]
    for coefficient in coefficients[-2::-1]:
        total = coefficient + value * total
    return total


def unit_circle(turns_times, multiple):
    turns = turns_times * np.float32(multiple / NFFT)
    magic = np.float32(1.5 * 2**23)
    part = turns - ((turns + magic) - magic)
    quarter = part * np.float32(0.25)
    square = quarter * quarter
    sine = quarter * horner(SINE, square)
    cosine = horner(COSINE, square)
    for _ in range(2):
        twice = sine + sine
        sine, cosine = twice * cosine, np.float32(1.0) - twice * sine
    return cosine, sine


def replica_tiles(tau):
    delay = tau.astype(f32)
    c0, s0 = unit_circle(delay, lowest_bin)
    cd, sd = unit_circle(delay, bin_spacing)
    cosines = [c0, c0 * cd - s0 * sd]
    sines = [s0, s0 * cd + c0 * sd]
    twice = cd + cd
    for _ in range(2, NF):
        cosines.append(twice * cosines[-1] - cosines[-2])
        sines.append(twice * sines[-1] - sines[-2])
    return cosines, sines


VMEM = pl.BlockSpec(memory_space=pltpu.VMEM)
BY_COLUMNS = (((1,), (1,)), ((), ()))


def product(left, right):
    return lax.dot_general(left, right, BY_COLUMNS, preferred_element_type=f32)


def thirds(values):
    high = values.astype(bf16)
    rest = values - high.astype(f32)
    middle = rest.astype(bf16)
    low = (rest - middle.astype(f32)).astype(bf16)
    return high, middle, low


def exact_product(ones, values):
    high, middle, low = thirds(values)
    return product(ones, high) + (product(ones, middle) + product(ones, low))


def replicas_kernel(place, travel_ref, after_ref, rep_ref, token_ref):
    block = pl.program_id(0)
    token_ref[...] = jnp.zeros_like(token_ref)

    def body(step, carry):
        rows = pl.ds(pl.multiple_of(step * TILE, TILE), TILE)
        for half in range(CH // 128):
            lanes = slice(half * 128, (half + 1) * 128)
            cosines, sines = replica_tiles(travel_ref[0, 0, rows, lanes].astype(jnp.int32))
            for f in range(NF):
                rep_ref[block, f, rows, lanes] = cosines[f].astype(bf16)
                rep_ref[block, f, rows, CH + half * 128 : CH + (half + 1) * 128] = sines[f].astype(bf16)
        return carry

    lax.fori_loop(0, ROWS // TILE, body, 0)


def replicas(place, travel, after, first, own):
    def index(i, p):
        return (p[first + i], p[8] if own else 0, 0, 0)

    return pl.pallas_call(
        replicas_kernel,
        grid_spec=pltpu.PrefetchScalarGridSpec(
            num_scalar_prefetch=1,
            grid=(4,),
            in_specs=[pl.BlockSpec((1, 1, ROWS, CH), index), VMEM],
            out_specs=[VMEM, VMEM],
        ),
        out_shape=[
            jax.ShapeDtypeStruct((4, NF, ROWS, 2 * CH), bf16),
            jax.ShapeDtypeStruct((8, 128), jnp.int32),
        ],
        cost_estimate=pl.CostEstimate(flops=4_500_000_000, bytes_accessed=1_000_000, transcendentals=0),
        compiler_params=pltpu.CompilerParams(vmem_limit_bytes=4 << 20),
        name=f"replicas_{int(own)}_{first}",
    )(place, travel, after)


def join_kernel(a_ref, b_ref, token_ref, out_ref):
    half = a_ref.shape[0]
    out_ref[0:half] = a_ref[...]
    out_ref[half : 2 * half] = b_ref[...]


def join(a, b, token):
    return pl.pallas_call(
        join_kernel,
        in_specs=[VMEM] * 3,
        out_specs=VMEM,
        out_shape=jax.ShapeDtypeStruct((2 * a.shape[0],) + a.shape[1:], a.dtype),
        cost_estimate=pl.CostEstimate(flops=0, bytes_accessed=100_000, transcendentals=0),
        compiler_params=pltpu.CompilerParams(vmem_limit_bytes=2 << 20),
        name=f"join_{a.shape[0]}",
    )(a, b, token)


def beams_kernel(a_ref, b_ref, wa_ref, wb_ref, na_ref, nb_ref, out_ref, *, slot):
    columns = [
        product(a_ref[slot, f], wa_ref[f]) + product(b_ref[slot, f], wb_ref[f]) for f in range(NF)
    ]
    out_ref[0:ROWS] = jnp.concatenate(columns, axis=1).astype(out_ref.dtype)
    if out_ref.shape[0] > ROWS:
        out_ref[ROWS : ROWS + NORM_ROWS] = na_ref[...] + nb_ref[...]


def beams_block(reps, weights, norms, step):
    own = STEPS[step] == (0, 0)
    rows = ROWS if own else ROWS + NORM_ROWS
    return pl.pallas_call(
        functools.partial(beams_kernel, slot=step % 4),
        in_specs=[VMEM] * 6,
        out_specs=VMEM,
        out_shape=jax.ShapeDtypeStruct((rows, NF * COLS), f32 if own else bf16),
        cost_estimate=pl.CostEstimate(flops=3_000_000_000, bytes_accessed=1_000_000, transcendentals=0),
        compiler_params=pltpu.CompilerParams(vmem_limit_bytes=4 << 20),
        name=f"beams_{step}",
    )(*reps, *weights, *norms)


def prepare_kernel(low_ref, high_ref, token_ref, w_ref, norm_ref, wide, *, first_row):
    for g in range(16):
        source = (low_ref, high_ref)[g // 8]
        for half in range(CH // 128):
            lanes = slice(half * 128, (half + 1) * 128)
            wide[half, g * 48 : (g + 1) * 48, :] = source[g % 8, :, lanes].astype(f32)
    squares = jnp.zeros((COLS, CH), f32)
    for f in range(NF):
        real, imag = [
            jnp.concatenate(
                [
                    jnp.concatenate(
                        [
                            wide[half, pl.ds(p * 24 + f * 3 + i, 16, stride=48), :]
                            for half in range(CH // 128)
                        ],
                        axis=1,
                    )
                    for i in range(3)
                ],
                axis=0,
            )
            for p in range(2)
        ]
        both = jnp.concatenate([real, imag], axis=0)
        squares = squares + both * both
        w_ref[f, :, 0:CH] = both.astype(bf16)
        w_ref[f, :, CH : 2 * CH] = jnp.concatenate([-imag, real], axis=0).astype(bf16)
    sums = exact_product(jnp.ones((NORM_ROWS, CH), bf16), squares)
    row = lax.broadcasted_iota(jnp.int32, sums.shape, 0) - first_row
    zero = jnp.zeros_like(sums)
    split = zero
    for index, part in enumerate(thirds(sums)):
        split = jnp.where(row == index, part.astype(f32), split)
    norm_ref[...] = jnp.concatenate([split] + [zero] * (NF - 1), axis=1).astype(bf16)


def prepare(low, high, token, first_row):
    return pl.pallas_call(
        functools.partial(prepare_kernel, first_row=first_row),
        in_specs=[VMEM] * 3,
        out_specs=[VMEM, VMEM],
        scratch_shapes=[pltpu.VMEM((CH // 128, 768, 128), f32)],
        out_shape=[
            jax.ShapeDtypeStruct((NF, COLS, 2 * CH), bf16),
            jax.ShapeDtypeStruct((NORM_ROWS, NF * COLS), bf16),
        ],
        cost_estimate=pl.CostEstimate(flops=1_000_000_000, bytes_accessed=1_000_000, transcendentals=0),
        compiler_params=pltpu.CompilerParams(vmem_limit_bytes=6 << 20),
        name=f"prepare_{first_row}",
    )(low, high, token)


def column_tables():
    slot = np.arange(NF * COLS) % 48
    place = slot % 16
    relative = sum(((place >> bit) & 1) << (3 - bit) for bit in range(4))
    return np.stack([relative, slot // 16]).astype(np.int32)


def finish_kernel(place, *refs, count):
    *received, own_ref, na_ref, nb_ref, table_ref, out_ref = refs
    window = lax.broadcasted_iota(jnp.int32, (48, NF * COLS), 0)
    source = table_ref[0:1, :] ^ place[9]
    pick = jnp.where(window == 3 * source + table_ref[1:2, :], 1.0, 0.0).astype(bf16)
    beams = own_ref[...]
    norm_rows = na_ref[...].astype(f32) + nb_ref[...].astype(f32)
    for ref in received:
        beams = beams + ref[0:ROWS].astype(f32)
        norm_rows = norm_rows + ref[ROWS : ROWS + NORM_ROWS].astype(f32)
    norm_sum = jnp.sum(exact_product(pick, norm_rows), axis=1, keepdims=True)
    window_norm = norm_sum / count + 1e-06
    out_ref[...] = exact_product(pick, beams * beams) / (count * window_norm)


def finish(place, received, own, norms, count):
    return pl.pallas_call(
        functools.partial(finish_kernel, count=count),
        in_specs=[pl.BlockSpec(memory_space=pltpu.SMEM)] + [VMEM] * 11,
        out_specs=VMEM,
        out_shape=jax.ShapeDtypeStruct((48, ROWS), f32),
        compiler_params=pltpu.CompilerParams(vmem_limit_bytes=8 << 20),
        name="finish",
    )(place, *received, own, *norms, jnp.asarray(column_tables()))


LAG = 3
STEPS = ((2, 1), (1, 1), (3, 1), (2, 0), (0, 1), (1, 0), (3, 0), (0, 0))
SWAP = [(0, 1), (1, 0)]


def tie(*values):
    return lax.optimization_barrier(values)


def per_device(spectra, travel, quality):
    x, yh, core = lax.axis_index("x"), lax.axis_index("yh"), lax.axis_index("c")
    order = [((x + dx) % 4) * 2 + (yh ^ dy) for dx, dy in STEPS]
    place = jnp.stack(order + [core, lax.axis_index("z") * 2 + lax.axis_index("yl")]).astype(jnp.int32)
    blocks = travel.reshape(8, 2, ROWS, CH)
    sent = lax.dynamic_slice(blocks, (0, 1 - core, 0, 0), (8, 1, ROWS, CH)).astype(jnp.int16)
    block = (spectra * quality.astype(bf16)).reshape(1, 48, CH)
    block, sent, place = tie(block, sent, place)

    def partner(mask):
        return [(i, i ^ mask) for i in range(16)]

    arrived = lax.ppermute(sent, "c", SWAP)
    held = block
    reps = []
    for stage, mask in enumerate((8, 4, 2, 1)):
        other = lax.ppermute(held, ("z", "yl"), partner(mask))
        if stage == 3:
            held_swapped = lax.ppermute(held, "c", SWAP)
        rep, token = replicas(place, blocks if stage < 2 else arrived, held, 4 * (stage % 2), stage < 2)
        reps.append(rep)
        if stage < 3:
            held = join(held, other, token)
    other_swapped = lax.ppermute(other, "c", SWAP)
    w_a, n_a = prepare(held, other, token, 0)
    w_b, n_b = prepare(held_swapped, other_swapped, token, 3)
    weights, norms = (w_a, w_b), (n_a, n_b)
    received = []
    for step, (dx, dy) in enumerate(STEPS):
        if step >= LAG:
            n_a, received[step - LAG] = tie(n_a, received[step - LAG])
        beams = beams_block((reps[step // 4], reps[2 + step // 4]), weights, (n_a, n_b), step)
        if (dx, dy) == (0, 0):
            kept = beams
        else:
            pairs = [(i, ((i // 2 + dx) % 4) * 2 + ((i % 2) ^ dy)) for i in range(8)]
            received.append(lax.ppermute(beams, ("x", "yh"), pairs))
    return finish(place, received, kept, (n_a, n_b), float(NF * CH * 16))


def solution(mesh):
    fine = Mesh(mesh.devices.reshape(8, 2, 4, 2, 2), ("z", "yl", "x", "yh", "c"))
    return jax.shard_map(
        per_device,
        mesh=fine,
        in_specs=(
            P(None, None, ("z", "yl"), ("x", "yh", "c")),
            P(("z", "yl"), ("x", "yh", "c")),
            P(("x", "yh", "c")),
        ),
        out_specs=P(None, ("z", "yl", "x", "yh", "c")),
        check_vma=False,
    )
```

```python
import functools

import jax
import jax.numpy as jnp
import numpy as np
from jax import lax
from jax.experimental import pallas as pl
from jax.experimental.pallas import tpu as pltpu
from jax.sharding import Mesh, PartitionSpec as P

NFFT = 2048
lowest_bin = 37
bin_spacing = 29
f32 = jnp.float32
bf16 = jnp.bfloat16

NF = 8
ROWS = 256
CH = 256
COLS = 96
TILE = 32
NORM_ROWS = 8


def series_coefficients():
    nodes = np.cos(np.linspace(0, np.pi, 4002)) / 8
    squares = nodes**2
    angles = 2 * np.pi * nodes
    sine = np.linalg.lstsq(squares[:, None] ** np.arange(4), np.sin(angles) / nodes, rcond=None)[0]
    cosine = np.linalg.lstsq(squares[:, None] ** np.arange(5), np.cos(angles), rcond=None)[0]
    return [np.float32(v) for v in sine], [np.float32(v) for v in cosine]


SINE, COSINE = series_coefficients()


def horner(coefficients, value):
    total = coefficients[-1]
    for coefficient in coefficients[-2::-1]:
        total = coefficient + value * total
    return total


def unit_circle(turns_times, multiple):
    turns = turns_times * np.float32(multiple / NFFT)
    magic = np.float32(1.5 * 2**23)
    part = turns - ((turns + magic) - magic)
    quarter = part * np.float32(0.25)
    square = quarter * quarter
    sine = quarter * horner(SINE, square)
    cosine = horner(COSINE, square)
    for _ in range(2):
        twice = sine + sine
        sine, cosine = twice * cosine, np.float32(1.0) - twice * sine
    return cosine, sine


def replica_tiles(tau):
    delay = tau.astype(f32)
    c0, s0 = unit_circle(delay, lowest_bin)
    cd, sd = unit_circle(delay, bin_spacing)
    cosines = [c0, c0 * cd - s0 * sd]
    sines = [s0, s0 * cd + c0 * sd]
    twice = cd + cd
    for _ in range(2, NF):
        cosines.append(twice * cosines[-1] - cosines[-2])
        sines.append(twice * sines[-1] - sines[-2])
    return cosines, sines


VMEM = pl.BlockSpec(memory_space=pltpu.VMEM)
BY_COLUMNS = (((1,), (1,)), ((), ()))


def product(left, right):
    return lax.dot_general(left, right, BY_COLUMNS, preferred_element_type=f32)


def thirds(values):
    high = values.astype(bf16)
    rest = values - high.astype(f32)
    middle = rest.astype(bf16)
    low = (rest - middle.astype(f32)).astype(bf16)
    return high, middle, low


def exact_product(ones, values):
    high, middle, low = thirds(values)
    return product(ones, high) + (product(ones, middle) + product(ones, low))


def replicas_kernel(place, travel_ref, after_ref, rep_ref, token_ref):
    block = pl.program_id(0)
    token_ref[...] = jnp.zeros_like(token_ref)

    def body(step, carry):
        rows = pl.ds(pl.multiple_of(step * TILE, TILE), TILE)
        for half in range(CH // 128):
            lanes = slice(half * 128, (half + 1) * 128)
            cosines, sines = replica_tiles(travel_ref[0, 0, rows, lanes].astype(jnp.int32))
            for f in range(NF):
                rep_ref[block, f, rows, lanes] = cosines[f].astype(bf16)
                rep_ref[block, f, rows, CH + half * 128 : CH + (half + 1) * 128] = sines[f].astype(bf16)
        return carry

    lax.fori_loop(0, ROWS // TILE, body, 0)


def replicas(place, travel, after, first, own):
    def index(i, p):
        return (p[first + i], 0, 0, 0)

    return pl.pallas_call(
        replicas_kernel,
        grid_spec=pltpu.PrefetchScalarGridSpec(
            num_scalar_prefetch=1,
            grid=(4,),
            in_specs=[pl.BlockSpec((1, 1, ROWS, CH), index), VMEM],
            out_specs=[VMEM, VMEM],
        ),
        out_shape=[
            jax.ShapeDtypeStruct((4, NF, ROWS, 2 * CH), bf16),
            jax.ShapeDtypeStruct((8, 128), jnp.int32),
        ],
        cost_estimate=pl.CostEstimate(flops=4_500_000_000, bytes_accessed=1_000_000, transcendentals=0),
        compiler_params=pltpu.CompilerParams(vmem_limit_bytes=4 << 20),
        name=f"replicas_{int(own)}_{first}",
    )(place, travel, after)


def join_kernel(a_ref, b_ref, token_ref, out_ref):
    half = a_ref.shape[0]
    out_ref[0:half] = a_ref[...]
    out_ref[half : 2 * half] = b_ref[...]


def join(a, b, token):
    return pl.pallas_call(
        join_kernel,
        in_specs=[VMEM] * 3,
        out_specs=VMEM,
        out_shape=jax.ShapeDtypeStruct((2 * a.shape[0],) + a.shape[1:], a.dtype),
        cost_estimate=pl.CostEstimate(flops=0, bytes_accessed=100_000, transcendentals=0),
        compiler_params=pltpu.CompilerParams(vmem_limit_bytes=2 << 20),
        name=f"join_{a.shape[0]}",
    )(a, b, token)


def beams_kernel(a_ref, b_ref, wa_ref, wb_ref, na_ref, nb_ref, out_ref, *, slot):
    columns = [
        product(a_ref[slot, f], wa_ref[f]) + product(b_ref[slot, f], wb_ref[f]) for f in range(NF)
    ]
    out_ref[0:ROWS] = jnp.concatenate(columns, axis=1).astype(out_ref.dtype)
    if out_ref.shape[0] > ROWS:
        out_ref[ROWS : ROWS + NORM_ROWS] = na_ref[...] + nb_ref[...]


def beams_block(reps, weights, norms, step):
    own = STEPS[step] == (0, 0)
    rows = ROWS if own else ROWS + NORM_ROWS
    return pl.pallas_call(
        functools.partial(beams_kernel, slot=step % 4),
        in_specs=[VMEM] * 6,
        out_specs=VMEM,
        out_shape=jax.ShapeDtypeStruct((rows, NF * COLS), f32 if own else bf16),
        cost_estimate=pl.CostEstimate(flops=3_000_000_000, bytes_accessed=1_000_000, transcendentals=0),
        compiler_params=pltpu.CompilerParams(vmem_limit_bytes=4 << 20),
        name=f"beams_{step}",
    )(*reps, *weights, *norms)


def prepare_kernel(low_ref, high_ref, token_ref, w_ref, norm_ref, wide, *, first_row):
    for g in range(16):
        source = (low_ref, high_ref)[g // 8]
        for half in range(CH // 128):
            lanes = slice(half * 128, (half + 1) * 128)
            wide[half, g * 48 : (g + 1) * 48, :] = source[g % 8, :, lanes].astype(f32)
    squares = jnp.zeros((COLS, CH), f32)
    for f in range(NF):
        real, imag = [
            jnp.concatenate(
                [
                    jnp.concatenate(
                        [
                            wide[half, pl.ds(p * 24 + f * 3 + i, 16, stride=48), :]
                            for half in range(CH // 128)
                        ],
                        axis=1,
                    )
                    for i in range(3)
                ],
                axis=0,
            )
            for p in range(2)
        ]
        both = jnp.concatenate([real, imag], axis=0)
        squares = squares + both * both
        w_ref[f, :, 0:CH] = both.astype(bf16)
        w_ref[f, :, CH : 2 * CH] = jnp.concatenate([-imag, real], axis=0).astype(bf16)
    sums = exact_product(jnp.ones((NORM_ROWS, CH), bf16), squares)
    row = lax.broadcasted_iota(jnp.int32, sums.shape, 0) - first_row
    zero = jnp.zeros_like(sums)
    split = zero
    for index, part in enumerate(thirds(sums)):
        split = jnp.where(row == index, part.astype(f32), split)
    norm_ref[...] = jnp.concatenate([split] + [zero] * (NF - 1), axis=1).astype(bf16)


def prepare(low, high, token, first_row):
    return pl.pallas_call(
        functools.partial(prepare_kernel, first_row=first_row),
        in_specs=[VMEM] * 3,
        out_specs=[VMEM, VMEM],
        scratch_shapes=[pltpu.VMEM((CH // 128, 768, 128), f32)],
        out_shape=[
            jax.ShapeDtypeStruct((NF, COLS, 2 * CH), bf16),
            jax.ShapeDtypeStruct((NORM_ROWS, NF * COLS), bf16),
        ],
        cost_estimate=pl.CostEstimate(flops=1_000_000_000, bytes_accessed=1_000_000, transcendentals=0),
        compiler_params=pltpu.CompilerParams(vmem_limit_bytes=6 << 20),
        name=f"prepare_{first_row}",
    )(low, high, token)


def column_tables():
    slot = np.arange(NF * COLS) % 48
    place = slot % 16
    relative = sum(((place >> bit) & 1) << (3 - bit) for bit in range(4))
    return np.stack([relative, slot // 16]).astype(np.int32)


def finish_kernel(place, *refs, count):
    *received, own_ref, na_ref, nb_ref, table_ref, out_ref = refs
    window = lax.broadcasted_iota(jnp.int32, (48, NF * COLS), 0)
    source = table_ref[0:1, :] ^ place[9]
    pick = jnp.where(window == 3 * source + table_ref[1:2, :], 1.0, 0.0).astype(bf16)
    beams = own_ref[...]
    norm_rows = na_ref[...].astype(f32) + nb_ref[...].astype(f32)
    for ref in received:
        beams = beams + ref[0:ROWS].astype(f32)
        norm_rows = norm_rows + ref[ROWS : ROWS + NORM_ROWS].astype(f32)
    norm_sum = jnp.sum(exact_product(pick, norm_rows), axis=1, keepdims=True)
    window_norm = norm_sum / count + 1e-06
    out_ref[...] = exact_product(pick, beams * beams) / (count * window_norm)


def finish(place, received, own, norms, count):
    return pl.pallas_call(
        functools.partial(finish_kernel, count=count),
        in_specs=[pl.BlockSpec(memory_space=pltpu.SMEM)] + [VMEM] * 11,
        out_specs=VMEM,
        out_shape=jax.ShapeDtypeStruct((48, ROWS), f32),
        compiler_params=pltpu.CompilerParams(vmem_limit_bytes=8 << 20),
        name="finish",
    )(place, *received, own, *norms, jnp.asarray(column_tables()))


LAG = 4
STEPS = ((2, 1), (1, 1), (3, 1), (2, 0), (0, 1), (1, 0), (3, 0), (0, 0))
SWAP = [(0, 1), (1, 0)]


def tie(*values):
    return lax.optimization_barrier(values)


def per_device(spectra, travel, quality):
    x, yh, core = lax.axis_index("x"), lax.axis_index("yh"), lax.axis_index("c")
    order = [((x + dx) % 4) * 2 + (yh ^ dy) for dx, dy in STEPS]
    place = jnp.stack(order + [core, lax.axis_index("z") * 2 + lax.axis_index("yl")]).astype(jnp.int32)
    blocks = travel.reshape(8, 2, ROWS, CH)
    block = (spectra * quality.astype(bf16)).reshape(1, 48, CH)
    kept_travel, sent = [
        lax.dynamic_slice(blocks, (0, of, 0, 0), (8, 1, ROWS, CH)).astype(jnp.int16)
        for of in (core, 1 - core)
    ]
    block, kept_travel, sent, place = tie(block, kept_travel, sent, place)

    def partner(mask):
        return [(i, i ^ mask) for i in range(16)]

    arrived = lax.ppermute(sent, "c", SWAP)
    held = block
    reps = {}
    for stage, mask in enumerate((8, 4, 2, 1)):
        other = lax.ppermute(held, ("z", "yl"), partner(mask))
        if stage == 3:
            held_swapped = lax.ppermute(held, "c", SWAP)
            break
        own, first = ((True, 0), (False, 0), (True, 4))[stage]
        reps[own, first], token = replicas(place, kept_travel if own else arrived, held, first, own)
        held = join(held, other, token)
    other_swapped = lax.ppermute(other, "c", SWAP)
    w_a, n_a = prepare(held, other, token, 0)
    w_b, n_b = prepare(held_swapped, other_swapped, token, 3)
    weights = (w_a, w_b)
    received = []
    for step, (dx, dy) in enumerate(STEPS):
        if step >= LAG:
            n_a, received[step - LAG] = tie(n_a, received[step - LAG])
        if step == 4:
            reps[False, 4], _ = replicas(place, arrived, beams, 4, False)
        first = step // 4 * 4
        beams = beams_block((reps[True, first], reps[False, first]), weights, (n_a, n_b), step)
        if (dx, dy) == (0, 0):
            kept = beams
        else:
            pairs = [(i, ((i // 2 + dx) % 4) * 2 + ((i % 2) ^ dy)) for i in range(8)]
            received.append(lax.ppermute(beams, ("x", "yh"), pairs))
    return finish(place, received, kept, (n_a, n_b), float(NF * CH * 16))


def solution(mesh):
    fine = Mesh(mesh.devices.reshape(8, 2, 4, 2, 2), ("z", "yl", "x", "yh", "c"))
    return jax.shard_map(
        per_device,
        mesh=fine,
        in_specs=(
            P(None, None, ("z", "yl"), ("x", "yh", "c")),
            P(("z", "yl"), ("x", "yh", "c")),
            P(("x", "yh", "c")),
        ),
        out_specs=P(None, ("z", "yl", "x", "yh", "c")),
        check_vma=False,
    )
```

```python
import functools

import jax
import jax.numpy as jnp
import numpy as np
from jax import lax
from jax.experimental import pallas as pl
from jax.experimental.pallas import tpu as pltpu
from jax.sharding import Mesh, PartitionSpec as P

NFFT = 2048
lowest_bin = 37
bin_spacing = 29
f32 = jnp.float32
bf16 = jnp.bfloat16

NF = 8
ROWS = 256
CH = 256
COLS = 96
TILE = 32
NORM_ROWS = 8


def series_coefficients():
    nodes = np.cos(np.linspace(0, np.pi, 4002)) / 8
    squares = nodes**2
    angles = 2 * np.pi * nodes
    sine = np.linalg.lstsq(squares[:, None] ** np.arange(4), np.sin(angles) / nodes, rcond=None)[0]
    cosine = np.linalg.lstsq(squares[:, None] ** np.arange(5), np.cos(angles), rcond=None)[0]
    return [np.float32(v) for v in sine], [np.float32(v) for v in cosine]


SINE, COSINE = series_coefficients()


def horner(coefficients, value):
    total = coefficients[-1]
    for coefficient in coefficients[-2::-1]:
        total = coefficient + value * total
    return total


def unit_circle(turns_times, multiple):
    turns = turns_times * np.float32(multiple / NFFT)
    magic = np.float32(1.5 * 2**23)
    part = turns - ((turns + magic) - magic)
    quarter = part * np.float32(0.25)
    square = quarter * quarter
    sine = quarter * horner(SINE, square)
    cosine = horner(COSINE, square)
    for _ in range(2):
        twice = sine + sine
        sine, cosine = twice * cosine, np.float32(1.0) - twice * sine
    return cosine, sine


def replica_tiles(tau):
    delay = tau.astype(f32)
    c0, s0 = unit_circle(delay, lowest_bin)
    cd, sd = unit_circle(delay, bin_spacing)
    cosines = [c0, c0 * cd - s0 * sd]
    sines = [s0, s0 * cd + c0 * sd]
    twice = cd + cd
    for _ in range(2, NF):
        cosines.append(twice * cosines[-1] - cosines[-2])
        sines.append(twice * sines[-1] - sines[-2])
    return cosines, sines


VMEM = pl.BlockSpec(memory_space=pltpu.VMEM)
BY_COLUMNS = (((1,), (1,)), ((), ()))


def product(left, right):
    return lax.dot_general(left, right, BY_COLUMNS, preferred_element_type=f32)


def thirds(values):
    high = values.astype(bf16)
    rest = values - high.astype(f32)
    middle = rest.astype(bf16)
    low = (rest - middle.astype(f32)).astype(bf16)
    return high, middle, low


def exact_product(ones, values):
    high, middle, low = thirds(values)
    return product(ones, high) + (product(ones, middle) + product(ones, low))


def replicas_kernel(place, travel_ref, after_ref, rep_ref, token_ref):
    block = pl.program_id(0)
    token_ref[...] = jnp.zeros_like(token_ref)

    def body(step, carry):
        rows = pl.ds(pl.multiple_of(step * TILE, TILE), TILE)
        for half in range(CH // 128):
            lanes = slice(half * 128, (half + 1) * 128)
            cosines, sines = replica_tiles(travel_ref[0, rows, lanes].astype(jnp.int32))
            for f in range(NF):
                rep_ref[block, f, rows, lanes] = cosines[f].astype(bf16)
                rep_ref[block, f, rows, CH + half * 128 : CH + (half + 1) * 128] = sines[f].astype(bf16)
        return carry

    lax.fori_loop(0, ROWS // TILE, body, 0)


def replicas(place, travel, after, name):
    def index(i, p):
        return (p[i], 0, 0)

    return pl.pallas_call(
        replicas_kernel,
        grid_spec=pltpu.PrefetchScalarGridSpec(
            num_scalar_prefetch=1,
            grid=(4,),
            in_specs=[pl.BlockSpec((1, ROWS, CH), index), VMEM],
            out_specs=[VMEM, VMEM],
        ),
        out_shape=[
            jax.ShapeDtypeStruct((4, NF, ROWS, 2 * CH), bf16),
            jax.ShapeDtypeStruct((8, 128), jnp.int32),
        ],
        cost_estimate=pl.CostEstimate(flops=40_000_000_000, bytes_accessed=1_000_000, transcendentals=0),
        compiler_params=pltpu.CompilerParams(vmem_limit_bytes=4 << 20),
        name=f"replicas_{name}",
    )(place, travel, after)


def join_kernel(a_ref, b_ref, token_ref, out_ref):
    half = a_ref.shape[0]
    out_ref[0:half] = a_ref[...]
    out_ref[half : 2 * half] = b_ref[...]


def join(a, b, token):
    return pl.pallas_call(
        join_kernel,
        in_specs=[VMEM] * 3,
        out_specs=VMEM,
        out_shape=jax.ShapeDtypeStruct((2 * a.shape[0],) + a.shape[1:], a.dtype),
        cost_estimate=pl.CostEstimate(flops=0, bytes_accessed=100_000, transcendentals=0),
        compiler_params=pltpu.CompilerParams(vmem_limit_bytes=2 << 20),
        name=f"join_{a.shape[0]}",
    )(a, b, token)


def beams_kernel(r0, r1, r2, r3, wa_ref, wb_ref, na_ref, nb_ref, out_ref, *, slot):
    columns = [
        (product(r0[slot, f], wa_ref[0, f]) + product(r1[slot, f], wb_ref[0, f]))
        + (product(r2[slot, f], wa_ref[1, f]) + product(r3[slot, f], wb_ref[1, f]))
        for f in range(NF)
    ]
    out_ref[0:ROWS] = jnp.concatenate(columns, axis=1).astype(out_ref.dtype)
    if out_ref.shape[0] > ROWS:
        out_ref[ROWS : ROWS + NORM_ROWS] = na_ref[...] + nb_ref[...]


def beams_block(reps, weights, norms, step):
    own = STEPS[step] == 0
    rows = ROWS if own else ROWS + NORM_ROWS
    return pl.pallas_call(
        functools.partial(beams_kernel, slot=step),
        in_specs=[VMEM] * 8,
        out_specs=VMEM,
        out_shape=jax.ShapeDtypeStruct((rows, NF * COLS), f32 if own else bf16),
        cost_estimate=pl.CostEstimate(flops=3_000_000_000, bytes_accessed=1_000_000, transcendentals=0),
        compiler_params=pltpu.CompilerParams(vmem_limit_bytes=4 << 20),
        name=f"beams_{step}",
    )(*reps, *weights, *norms)


def prepare_kernel(low_ref, high_ref, w_ref, norm_ref, wide, *, first_row):
    squares = jnp.zeros((COLS, CH), f32)
    for flip in range(2):
        for g in range(16):
            source = (low_ref, high_ref)[g // 8]
            for half in range(CH // 128):
                lanes = slice(half * 128, (half + 1) * 128)
                wide[half, g * 48 : (g + 1) * 48, :] = source[flip * 8 + g % 8, :, lanes].astype(f32)
        for f in range(NF):
            real, imag = [
                jnp.concatenate(
                    [
                        jnp.concatenate(
                            [
                                wide[half, pl.ds(p * 24 + f * 3 + i, 16, stride=48), :]
                                for half in range(CH // 128)
                            ],
                            axis=1,
                        )
                        for i in range(3)
                    ],
                    axis=0,
                )
                for p in range(2)
            ]
            both = jnp.concatenate([real, imag], axis=0)
            squares = squares + both * both
            w_ref[flip, f, :, 0:CH] = both.astype(bf16)
            w_ref[flip, f, :, CH : 2 * CH] = jnp.concatenate([-imag, real], axis=0).astype(bf16)
    sums = exact_product(jnp.ones((NORM_ROWS, CH), bf16), squares)
    row = lax.broadcasted_iota(jnp.int32, sums.shape, 0) - first_row
    zero = jnp.zeros_like(sums)
    split = zero
    for index, part in enumerate(thirds(sums)):
        split = jnp.where(row == index, part.astype(f32), split)
    norm_ref[...] = jnp.concatenate([split] + [zero] * (NF - 1), axis=1).astype(bf16)


def prepare(low, high, first_row):
    return pl.pallas_call(
        functools.partial(prepare_kernel, first_row=first_row),
        in_specs=[VMEM] * 2,
        out_specs=[VMEM, VMEM],
        scratch_shapes=[pltpu.VMEM((CH // 128, 768, 128), f32)],
        out_shape=[
            jax.ShapeDtypeStruct((2, NF, COLS, 2 * CH), bf16),
            jax.ShapeDtypeStruct((NORM_ROWS, NF * COLS), bf16),
        ],
        cost_estimate=pl.CostEstimate(flops=1_000_000_000, bytes_accessed=1_000_000, transcendentals=0),
        compiler_params=pltpu.CompilerParams(vmem_limit_bytes=6 << 20),
        name=f"prepare_{first_row}",
    )(low, high)


def column_tables():
    slot = np.arange(NF * COLS) % 48
    place = slot % 16
    relative = sum(((place >> bit) & 1) * mask for bit, mask in enumerate((8, 4, 1, 2)))
    return np.stack([relative, slot // 16]).astype(np.int32)


def finish_kernel(place, *refs, count):
    *received, own_ref, na_ref, nb_ref, table_ref, out_ref = refs
    window = lax.broadcasted_iota(jnp.int32, (48, NF * COLS), 0)
    source = table_ref[0:1, :] ^ place[4]
    pick = jnp.where(window == 3 * source + table_ref[1:2, :], 1.0, 0.0).astype(bf16)
    beams = own_ref[...]
    norm_rows = na_ref[...].astype(f32) + nb_ref[...].astype(f32)
    for ref in received:
        beams = beams + ref[0:ROWS].astype(f32)
        norm_rows = norm_rows + ref[ROWS : ROWS + NORM_ROWS].astype(f32)
    norm_sum = jnp.sum(exact_product(pick, norm_rows), axis=1, keepdims=True)
    window_norm = norm_sum / count + 1e-06
    out_ref[...] = exact_product(pick, beams * beams) / (count * window_norm)


def finish(place, received, own, norms, count):
    return pl.pallas_call(
        functools.partial(finish_kernel, count=count),
        in_specs=[pl.BlockSpec(memory_space=pltpu.SMEM)] + [VMEM] * 7,
        out_specs=VMEM,
        out_shape=jax.ShapeDtypeStruct((48, ROWS), f32),
        compiler_params=pltpu.CompilerParams(vmem_limit_bytes=8 << 20),
        name="finish",
    )(place, *received, own, *norms, jnp.asarray(column_tables()))


STEPS = (2, 1, 3, 0)
SWAP = [(0, 1), (1, 0)]


def tie(*values):
    return lax.optimization_barrier(values)


def per_device(spectra, travel, quality):
    x, yh, core = lax.axis_index("x"), lax.axis_index("yh"), lax.axis_index("c")
    order = [(x + dx) % 4 for dx in STEPS]
    place = jnp.stack(order + [lax.axis_index("z") * 2 + lax.axis_index("yl")]).astype(jnp.int32)
    blocks = travel.reshape(4, 2, 2, ROWS, CH)

    def travel_for(flip_y, flip_c):
        return lax.dynamic_slice(
            blocks, (0, yh ^ flip_y, core ^ flip_c, 0, 0), (4, 1, 1, ROWS, CH)
        ).reshape(4, ROWS, CH).astype(jnp.int16)

    block = (spectra * quality.astype(bf16)).reshape(1, 48, CH)
    parts = [travel_for(flip // 2, flip % 2) for flip in range(4)]
    block, place, *parts = tie(block, place, *parts)

    def moved(flip):
        return lax.ppermute(parts[flip], ("yh", "c"), [(i, i ^ flip) for i in range(4)])

    def exchange(values, stage):
        if stage == 3:
            return lax.ppermute(values, "yh", SWAP)
        mask = (8, 4, 1, None, 2)[stage]
        return lax.ppermute(values, ("z", "yl"), [(i, i ^ mask) for i in range(16)])

    far, near, both = moved(2), moved(1), moved(3)
    held = block
    other = exchange(held, 0)
    rep_own, token = replicas(place, parts[0], held, "own")
    held = join(held, other, token)
    other = exchange(held, 1)
    rep_near, token = replicas(place, near, held, "near")
    held = join(held, other, token)
    for stage in (2, 3):
        other = exchange(held, stage)
        held = join(held, other, token)
    held, far, both = tie(held, far, both)
    other = exchange(held, 4)
    held_swapped = lax.ppermute(held, "c", SWAP)
    rep_far, token = replicas(place, far, held, "far")
    other_swapped = lax.ppermute(other, "c", SWAP)
    rep_both, _ = replicas(place, both, other, "both")
    w_a, n_a = prepare(held, other, 0)
    w_b, n_b = prepare(held_swapped, other_swapped, 3)
    reps = (rep_own, rep_near, rep_far, rep_both)
    received = []
    for step, dx in enumerate(STEPS):
        if step == 3:
            n_a, received[0] = tie(n_a, received[0])
        beams = beams_block(reps, (w_a, w_b), (n_a, n_b), step)
        if dx:
            received.append(lax.ppermute(beams, "x", [(i, (i + dx) % 4) for i in range(4)]))
    return finish(place, received, beams, (n_a, n_b), float(NF * CH * 16))


def solution(mesh):
    fine = Mesh(mesh.devices.reshape(8, 2, 4, 2, 2), ("z", "yl", "x", "yh", "c"))
    return jax.shard_map(
        per_device,
        mesh=fine,
        in_specs=(
            P(None, None, ("z", "yl"), ("x", "yh", "c")),
            P(("z", "yl"), ("x", "yh", "c")),
            P(("x", "yh", "c")),
        ),
        out_specs=P(None, ("z", "yl", "x", "yh", "c")),
        check_vma=False,
    )
```

```python
import functools

import jax
import jax.numpy as jnp
import numpy as np
from jax import lax
from jax.experimental import pallas as pl
from jax.experimental.pallas import tpu as pltpu
from jax.sharding import Mesh, PartitionSpec as P

NFFT = 2048
lowest_bin = 37
bin_spacing = 29
f32 = jnp.float32
bf16 = jnp.bfloat16

NF = 8
ROWS = 256
CH = 256
COLS = 96
TILE = 32
NORM_ROWS = 16


def series_coefficients():
    nodes = np.cos(np.linspace(0, np.pi, 4002)) / 8
    squares = nodes**2
    angles = 2 * np.pi * nodes
    sine = np.linalg.lstsq(squares[:, None] ** np.arange(4), np.sin(angles) / nodes, rcond=None)[0]
    cosine = np.linalg.lstsq(squares[:, None] ** np.arange(5), np.cos(angles), rcond=None)[0]
    return [np.float32(v) for v in sine], [np.float32(v) for v in cosine]


SINE, COSINE = series_coefficients()


def horner(coefficients, value):
    total = coefficients[-1]
    for coefficient in coefficients[-2::-1]:
        total = coefficient + value * total
    return total


def unit_circle(turns_times, multiple):
    turns = turns_times * np.float32(multiple / NFFT)
    magic = np.float32(1.5 * 2**23)
    part = turns - ((turns + magic) - magic)
    quarter = part * np.float32(0.25)
    square = quarter * quarter
    sine = quarter * horner(SINE, square)
    cosine = horner(COSINE, square)
    for _ in range(2):
        twice = sine + sine
        sine, cosine = twice * cosine, np.float32(1.0) - twice * sine
    return cosine, sine


def replica_tiles(tau):
    delay = tau.astype(f32)
    c0, s0 = unit_circle(delay, lowest_bin)
    cd, sd = unit_circle(delay, bin_spacing)
    cosines = [c0, c0 * cd - s0 * sd]
    sines = [s0, s0 * cd + c0 * sd]
    twice = cd + cd
    for _ in range(2, NF):
        cosines.append(twice * cosines[-1] - cosines[-2])
        sines.append(twice * sines[-1] - sines[-2])
    return cosines, sines


VMEM = pl.BlockSpec(memory_space=pltpu.VMEM)
BY_COLUMNS = (((1,), (1,)), ((), ()))


def product(left, right):
    return lax.dot_general(left, right, BY_COLUMNS, preferred_element_type=f32)


def thirds(values):
    high = values.astype(bf16)
    rest = values - high.astype(f32)
    middle = rest.astype(bf16)
    low = (rest - middle.astype(f32)).astype(bf16)
    return high, middle, low


def exact_product(ones, values):
    high, middle, low = thirds(values)
    return product(ones, high) + (product(ones, middle) + product(ones, low))


def replicas_kernel(place, travel_ref, after_ref, rep_ref, token_ref):
    block = pl.program_id(0)
    token_ref[...] = jnp.zeros_like(token_ref)

    def body(step, carry):
        rows = pl.ds(pl.multiple_of(step * TILE, TILE), TILE)
        for half in range(CH // 128):
            lanes = slice(half * 128, (half + 1) * 128)
            cosines, sines = replica_tiles(travel_ref[0, rows, lanes].astype(jnp.int32))
            for f in range(NF):
                rep_ref[block, f, rows, lanes] = cosines[f].astype(bf16)
                rep_ref[block, f, rows, CH + half * 128 : CH + (half + 1) * 128] = sines[f].astype(bf16)
        return carry

    lax.fori_loop(0, ROWS // TILE, body, 0)


def replicas(place, travel, after, name):
    def index(i, p):
        return (p[i], 0, 0)

    return pl.pallas_call(
        replicas_kernel,
        grid_spec=pltpu.PrefetchScalarGridSpec(
            num_scalar_prefetch=1,
            grid=(4,),
            in_specs=[pl.BlockSpec((1, ROWS, CH), index), VMEM],
            out_specs=[VMEM, VMEM],
        ),
        out_shape=[
            jax.ShapeDtypeStruct((4, NF, ROWS, 2 * CH), bf16),
            jax.ShapeDtypeStruct((8, 128), jnp.int32),
        ],
        cost_estimate=pl.CostEstimate(flops=40_000_000_000, bytes_accessed=1_000_000, transcendentals=0),
        compiler_params=pltpu.CompilerParams(vmem_limit_bytes=4 << 20),
        name=f"replicas_{name}",
    )(place, travel, after)


def join_kernel(a_ref, b_ref, token_ref, out_ref):
    half = a_ref.shape[0]
    out_ref[0:half] = a_ref[...]
    out_ref[half : 2 * half] = b_ref[...]


def join(a, b, token):
    return pl.pallas_call(
        join_kernel,
        in_specs=[VMEM] * 3,
        out_specs=VMEM,
        out_shape=jax.ShapeDtypeStruct((2 * a.shape[0],) + a.shape[1:], a.dtype),
        cost_estimate=pl.CostEstimate(flops=0, bytes_accessed=100_000, transcendentals=0),
        compiler_params=pltpu.CompilerParams(vmem_limit_bytes=2 << 20),
        name=f"join_{a.shape[0]}",
    )(a, b, token)


def beams_kernel(*refs, slot):
    reps, weights, norms, out_ref = refs[0:4], refs[4:8], refs[8:12], refs[12]
    columns = []
    for f in range(NF):
        parts = [product(rep[slot, f], w_ref[f]) for rep, w_ref in zip(reps, weights)]
        columns.append((parts[0] + parts[1]) + (parts[2] + parts[3]))
    out_ref[0:ROWS] = jnp.concatenate(columns, axis=1).astype(out_ref.dtype)
    if out_ref.shape[0] > ROWS:
        out_ref[ROWS : ROWS + NORM_ROWS] = (norms[0][...] + norms[1][...]) + (norms[2][...] + norms[3][...])


def beams_block(reps, weights, norms, step):
    own = STEPS[step] == 0
    rows = ROWS if own else ROWS + NORM_ROWS
    return pl.pallas_call(
        functools.partial(beams_kernel, slot=step),
        in_specs=[VMEM] * 12,
        out_specs=VMEM,
        out_shape=jax.ShapeDtypeStruct((rows, NF * COLS), f32 if own else bf16),
        cost_estimate=pl.CostEstimate(flops=3_000_000_000, bytes_accessed=1_000_000, transcendentals=0),
        compiler_params=pltpu.CompilerParams(vmem_limit_bytes=4 << 20),
        name=f"beams_{step}",
    )(*reps, *weights, *norms)


def prepare_kernel(source_ref, w_ref, norm_ref, wide, *, first_row):
    for g in range(16):
        for half in range(CH // 128):
            lanes = slice(half * 128, (half + 1) * 128)
            wide[half, g * 48 : (g + 1) * 48, :] = source_ref[g, :, lanes].astype(f32)
    squares = jnp.zeros((COLS, CH), f32)
    for f in range(NF):
        real, imag = [
            jnp.concatenate(
                [
                    jnp.concatenate(
                        [
                            wide[half, pl.ds(p * 24 + f * 3 + i, 16, stride=48), :]
                            for half in range(CH // 128)
                        ],
                        axis=1,
                    )
                    for i in range(3)
                ],
                axis=0,
            )
            for p in range(2)
        ]
        both = jnp.concatenate([real, imag], axis=0)
        squares = squares + both * both
        w_ref[f, :, 0:CH] = both.astype(bf16)
        w_ref[f, :, CH : 2 * CH] = jnp.concatenate([-imag, real], axis=0).astype(bf16)
    sums = exact_product(jnp.ones((NORM_ROWS, CH), bf16), squares)
    row = lax.broadcasted_iota(jnp.int32, sums.shape, 0) - first_row
    zero = jnp.zeros_like(sums)
    split = zero
    for index, part in enumerate(thirds(sums)):
        split = jnp.where(row == index, part.astype(f32), split)
    norm_ref[...] = jnp.concatenate([split] + [zero] * (NF - 1), axis=1).astype(bf16)


def prepare(source, first_row):
    return pl.pallas_call(
        functools.partial(prepare_kernel, first_row=first_row),
        in_specs=[VMEM],
        out_specs=[VMEM, VMEM],
        scratch_shapes=[pltpu.VMEM((CH // 128, 768, 128), f32)],
        out_shape=[
            jax.ShapeDtypeStruct((NF, COLS, 2 * CH), bf16),
            jax.ShapeDtypeStruct((NORM_ROWS, NF * COLS), bf16),
        ],
        cost_estimate=pl.CostEstimate(flops=1_000_000_000, bytes_accessed=1_000_000, transcendentals=0),
        compiler_params=pltpu.CompilerParams(vmem_limit_bytes=6 << 20),
        name=f"prepare_{first_row}",
    )(source)


def column_tables():
    slot = np.arange(NF * COLS) % 48
    place = slot % 16
    relative = sum(((place >> bit) & 1) * mask for bit, mask in enumerate((8, 4, 2, 1)))
    return np.stack([relative, slot // 16]).astype(np.int32)


def finish_kernel(place, *refs, count):
    received, own_ref, norms, table_ref, out_ref = refs[0:3], refs[3], refs[4:8], refs[8], refs[9]
    window = lax.broadcasted_iota(jnp.int32, (48, NF * COLS), 0)
    source = table_ref[0:1, :] ^ place[4]
    pick = jnp.where(window == 3 * source + table_ref[1:2, :], 1.0, 0.0).astype(bf16)
    beams = own_ref[...]
    norm_rows = sum(ref[...].astype(f32) for ref in norms)
    for ref in received:
        beams = beams + ref[0:ROWS].astype(f32)
        norm_rows = norm_rows + ref[ROWS : ROWS + NORM_ROWS].astype(f32)
    norm_sum = jnp.sum(exact_product(pick, norm_rows), axis=1, keepdims=True)
    window_norm = norm_sum / count + 1e-06
    out_ref[...] = exact_product(pick, beams * beams) / (count * window_norm)


def finish(place, received, own, norms, count):
    return pl.pallas_call(
        functools.partial(finish_kernel, count=count),
        in_specs=[pl.BlockSpec(memory_space=pltpu.SMEM)] + [VMEM] * 9,
        out_specs=VMEM,
        out_shape=jax.ShapeDtypeStruct((48, ROWS), f32),
        compiler_params=pltpu.CompilerParams(vmem_limit_bytes=8 << 20),
        name="finish",
    )(place, *received, own, *norms, jnp.asarray(column_tables()))


STEPS = (2, 1, 3, 0)
SWAP = [(0, 1), (1, 0)]


def tie(*values):
    return lax.optimization_barrier(values)


def per_device(spectra, travel, quality):
    x, yh, core = lax.axis_index("x"), lax.axis_index("yh"), lax.axis_index("c")
    order = [(x + dx) % 4 for dx in STEPS]
    place = jnp.stack(order + [lax.axis_index("z") * 2 + lax.axis_index("yl")]).astype(jnp.int32)
    blocks = travel.reshape(4, 2, 2, ROWS, CH)

    def travel_for(flip_y, flip_c):
        return lax.dynamic_slice(
            blocks, (0, yh ^ flip_y, core ^ flip_c, 0, 0), (4, 1, 1, ROWS, CH)
        ).reshape(4, ROWS, CH).astype(jnp.int16)

    block = (spectra * quality.astype(bf16)).reshape(1, 48, CH)
    parts = [travel_for(flip // 2, flip % 2) for flip in range(4)]
    place, *parts = tie(place, *parts)

    def moved(flip):
        return lax.ppermute(parts[flip], ("yh", "c"), [(i, i ^ flip) for i in range(4)])

    def exchange(values, stage):
        if stage == 4:
            return lax.ppermute(values, "yh", SWAP)
        mask = (8, 4, 2, 1)[stage]
        return lax.ppermute(values, ("z", "yl"), [(i, i ^ mask) for i in range(16)])

    far, near, both = moved(2), moved(1), moved(3)
    held = block
    other = exchange(held, 0)
    rep_own, token = replicas(place, parts[0], held, "own")
    held = join(held, other, token)
    other = exchange(held, 1)
    rep_near, token = replicas(place, near, held, "near")
    held = join(held, other, token)
    for stage in (2, 3):
        other = exchange(held, stage)
        held = join(held, other, token)
    held, far, both = tie(held, far, both)
    other = exchange(held, 4)
    held_swapped = lax.ppermute(held, "c", SWAP)
    rep_far, token = replicas(place, far, held, "far")
    other_swapped = lax.ppermute(other, "c", SWAP)
    rep_both, _ = replicas(place, both, other, "both")
    sources = (held, held_swapped, other, other_swapped)
    prepared = [prepare(source, 4 * index) for index, source in enumerate(sources)]
    weights, norms = [w for w, _ in prepared], [n for _, n in prepared]
    reps = (rep_own, rep_near, rep_far, rep_both)
    received = []
    for step, dx in enumerate(STEPS):
        if step == 3:
            norms[0], received[0] = tie(norms[0], received[0])
        beams = beams_block(reps, weights, norms, step)
        if dx:
            received.append(lax.ppermute(beams, "x", [(i, (i + dx) % 4) for i in range(4)]))
    return finish(place, received, beams, norms, float(NF * CH * 16))


def solution(mesh):
    fine = Mesh(mesh.devices.reshape(8, 2, 4, 2, 2), ("z", "yl", "x", "yh", "c"))
    return jax.shard_map(
        per_device,
        mesh=fine,
        in_specs=(
            P(None, None, ("z", "yl"), ("x", "yh", "c")),
            P(("z", "yl"), ("x", "yh", "c")),
            P(("x", "yh", "c")),
        ),
        out_specs=P(None, ("z", "yl", "x", "yh", "c")),
        check_vma=False,
    )
```

```python
import functools

import jax
import jax.numpy as jnp
import numpy as np
from jax import lax
from jax.experimental import pallas as pl
from jax.experimental.pallas import tpu as pltpu
from jax.sharding import Mesh, PartitionSpec as P

NFFT = 2048
lowest_bin = 37
bin_spacing = 29
f32 = jnp.float32
bf16 = jnp.bfloat16

NF = 8
ROWS = 256
CH = 256
COLS = 96
TILE = 32
NORM_ROWS = 16


def series_coefficients():
    nodes = np.cos(np.linspace(0, np.pi, 4002)) / 8
    squares = nodes**2
    angles = 2 * np.pi * nodes
    sine = np.linalg.lstsq(squares[:, None] ** np.arange(4), np.sin(angles) / nodes, rcond=None)[0]
    cosine = np.linalg.lstsq(squares[:, None] ** np.arange(5), np.cos(angles), rcond=None)[0]
    return [np.float32(v) for v in sine], [np.float32(v) for v in cosine]


SINE, COSINE = series_coefficients()


def horner(coefficients, value):
    total = coefficients[-1]
    for coefficient in coefficients[-2::-1]:
        total = coefficient + value * total
    return total


def unit_circle(turns_times, multiple):
    turns = turns_times * np.float32(multiple / NFFT)
    magic = np.float32(1.5 * 2**23)
    part = turns - ((turns + magic) - magic)
    quarter = part * np.float32(0.25)
    square = quarter * quarter
    sine = quarter * horner(SINE, square)
    cosine = horner(COSINE, square)
    for _ in range(2):
        twice = sine + sine
        sine, cosine = twice * cosine, np.float32(1.0) - twice * sine
    return cosine, sine


def replica_tiles(tau):
    delay = tau.astype(f32)
    c0, s0 = unit_circle(delay, lowest_bin)
    cd, sd = unit_circle(delay, bin_spacing)
    cosines = [c0, c0 * cd - s0 * sd]
    sines = [s0, s0 * cd + c0 * sd]
    twice = cd + cd
    for _ in range(2, NF):
        cosines.append(twice * cosines[-1] - cosines[-2])
        sines.append(twice * sines[-1] - sines[-2])
    return cosines, sines


VMEM = pl.BlockSpec(memory_space=pltpu.VMEM)
BY_COLUMNS = (((1,), (1,)), ((), ()))


def product(left, right):
    return lax.dot_general(left, right, BY_COLUMNS, preferred_element_type=f32)


def thirds(values):
    high = values.astype(bf16)
    rest = values - high.astype(f32)
    middle = rest.astype(bf16)
    low = (rest - middle.astype(f32)).astype(bf16)
    return high, middle, low


def exact_product(ones, values):
    high, middle, low = thirds(values)
    return product(ones, high) + (product(ones, middle) + product(ones, low))


def replicas_kernel(place, travel_ref, after_ref, rep_ref, token_ref):
    block = pl.program_id(0)
    token_ref[...] = jnp.zeros_like(token_ref)

    def body(step, carry):
        rows = pl.ds(pl.multiple_of(step * TILE, TILE), TILE)
        for half in range(CH // 128):
            lanes = slice(half * 128, (half + 1) * 128)
            cosines, sines = replica_tiles(travel_ref[0, rows, lanes].astype(jnp.int32))
            for f in range(NF):
                rep_ref[block, f, rows, lanes] = cosines[f].astype(bf16)
                rep_ref[block, f, rows, CH + half * 128 : CH + (half + 1) * 128] = sines[f].astype(bf16)
        return carry

    lax.fori_loop(0, ROWS // TILE, body, 0)


def replicas(place, travel, after, name):
    def index(i, p):
        return (p[i], 0, 0)

    return pl.pallas_call(
        replicas_kernel,
        grid_spec=pltpu.PrefetchScalarGridSpec(
            num_scalar_prefetch=1,
            grid=(4,),
            in_specs=[pl.BlockSpec((1, ROWS, CH), index), VMEM],
            out_specs=[VMEM, VMEM],
        ),
        out_shape=[
            jax.ShapeDtypeStruct((4, NF, ROWS, 2 * CH), bf16),
            jax.ShapeDtypeStruct((8, 128), jnp.int32),
        ],
        cost_estimate=pl.CostEstimate(flops=40_000_000_000, bytes_accessed=1_000_000, transcendentals=0),
        compiler_params=pltpu.CompilerParams(vmem_limit_bytes=4 << 20),
        name=f"replicas_{name}",
    )(place, travel, after)


def join_kernel(a_ref, b_ref, token_ref, out_ref):
    half = a_ref.shape[0]
    out_ref[0:half] = a_ref[...]
    out_ref[half : 2 * half] = b_ref[...]


def join(a, b, token):
    return pl.pallas_call(
        join_kernel,
        in_specs=[VMEM] * 3,
        out_specs=VMEM,
        out_shape=jax.ShapeDtypeStruct((2 * a.shape[0],) + a.shape[1:], a.dtype),
        cost_estimate=pl.CostEstimate(flops=0, bytes_accessed=100_000, transcendentals=0),
        compiler_params=pltpu.CompilerParams(vmem_limit_bytes=2 << 20),
        name=f"join_{a.shape[0]}",
    )(a, b, token)


def beams_kernel(*refs, slot):
    reps, weights, norms, out_ref = refs[0:4], refs[4:8], refs[8:12], refs[12]
    columns = []
    for f in range(NF):
        parts = [product(rep[slot, f], w_ref[f]) for rep, w_ref in zip(reps, weights)]
        columns.append((parts[0] + parts[1]) + (parts[2] + parts[3]))
    out_ref[0:ROWS] = jnp.concatenate(columns, axis=1).astype(out_ref.dtype)
    if out_ref.shape[0] > ROWS:
        out_ref[ROWS : ROWS + NORM_ROWS] = (norms[0][...] + norms[1][...]) + (norms[2][...] + norms[3][...])


def beams_block(reps, weights, norms, step):
    own = STEPS[step] == 0
    rows = ROWS if own else ROWS + NORM_ROWS
    return pl.pallas_call(
        functools.partial(beams_kernel, slot=step),
        in_specs=[VMEM] * 12,
        out_specs=VMEM,
        out_shape=jax.ShapeDtypeStruct((rows, NF * COLS), f32 if own else bf16),
        cost_estimate=pl.CostEstimate(flops=3_000_000_000, bytes_accessed=1_000_000, transcendentals=0),
        compiler_params=pltpu.CompilerParams(vmem_limit_bytes=4 << 20),
        name=f"beams_{step}",
    )(*reps, *weights, *norms)


def prepare_kernel(low_ref, high_ref, w_ref, norm_ref, wide, *, flip, first_row):
    for g in range(16):
        source_ref = (low_ref, high_ref)[g // 8]
        for half in range(CH // 128):
            lanes = slice(half * 128, (half + 1) * 128)
            wide[half, g * 48 : (g + 1) * 48, :] = source_ref[2 * (g % 8) + flip, :, lanes].astype(f32)
    squares = jnp.zeros((COLS, CH), f32)
    for f in range(NF):
        real, imag = [
            jnp.concatenate(
                [
                    jnp.concatenate(
                        [
                            wide[half, pl.ds(p * 24 + f * 3 + i, 16, stride=48), :]
                            for half in range(CH // 128)
                        ],
                        axis=1,
                    )
                    for i in range(3)
                ],
                axis=0,
            )
            for p in range(2)
        ]
        both = jnp.concatenate([real, imag], axis=0)
        squares = squares + both * both
        w_ref[f, :, 0:CH] = both.astype(bf16)
        w_ref[f, :, CH : 2 * CH] = jnp.concatenate([-imag, real], axis=0).astype(bf16)
    sums = exact_product(jnp.ones((NORM_ROWS, CH), bf16), squares)
    row = lax.broadcasted_iota(jnp.int32, sums.shape, 0) - first_row
    zero = jnp.zeros_like(sums)
    split = zero
    for index, part in enumerate(thirds(sums)):
        split = jnp.where(row == index, part.astype(f32), split)
    norm_ref[...] = jnp.concatenate([split] + [zero] * (NF - 1), axis=1).astype(bf16)


def prepare(low, high, flip, first_row):
    return pl.pallas_call(
        functools.partial(prepare_kernel, flip=flip, first_row=first_row),
        in_specs=[VMEM] * 2,
        out_specs=[VMEM, VMEM],
        scratch_shapes=[pltpu.VMEM((CH // 128, 768, 128), f32)],
        out_shape=[
            jax.ShapeDtypeStruct((NF, COLS, 2 * CH), bf16),
            jax.ShapeDtypeStruct((NORM_ROWS, NF * COLS), bf16),
        ],
        cost_estimate=pl.CostEstimate(flops=1_000_000_000, bytes_accessed=1_000_000, transcendentals=0),
        compiler_params=pltpu.CompilerParams(vmem_limit_bytes=6 << 20),
        name=f"prepare_{first_row}",
    )(low, high)


def column_tables():
    slot = np.arange(NF * COLS) % 48
    place = slot % 16
    relative = sum(((place >> bit) & 1) * mask for bit, mask in enumerate((1, 8, 4, 2)))
    return np.stack([relative, slot // 16]).astype(np.int32)


def finish_kernel(place, *refs, count):
    received, own_ref, norms, table_ref, out_ref = refs[0:3], refs[3], refs[4:8], refs[8], refs[9]
    window = lax.broadcasted_iota(jnp.int32, (48, NF * COLS), 0)
    source = table_ref[0:1, :] ^ place[4]
    pick = jnp.where(window == 3 * source + table_ref[1:2, :], 1.0, 0.0).astype(bf16)
    beams = own_ref[...]
    norm_rows = sum(ref[...].astype(f32) for ref in norms)
    for ref in received:
        beams = beams + ref[0:ROWS].astype(f32)
        norm_rows = norm_rows + ref[ROWS : ROWS + NORM_ROWS].astype(f32)
    norm_sum = jnp.sum(exact_product(pick, norm_rows), axis=1, keepdims=True)
    window_norm = norm_sum / count + 1e-06
    out_ref[...] = exact_product(pick, beams * beams) / (count * window_norm)


def finish(place, received, own, norms, count):
    return pl.pallas_call(
        functools.partial(finish_kernel, count=count),
        in_specs=[pl.BlockSpec(memory_space=pltpu.SMEM)] + [VMEM] * 9,
        out_specs=VMEM,
        out_shape=jax.ShapeDtypeStruct((48, ROWS), f32),
        compiler_params=pltpu.CompilerParams(vmem_limit_bytes=8 << 20),
        name="finish",
    )(place, *received, own, *norms, jnp.asarray(column_tables()))


STEPS = (2, 1, 3, 0)
SWAP = [(0, 1), (1, 0)]


def tie(*values):
    return lax.optimization_barrier(values)


def per_device(spectra, travel, quality):
    x, yh, core = lax.axis_index("x"), lax.axis_index("yh"), lax.axis_index("c")
    order = [(x + dx) % 4 for dx in STEPS]
    place = jnp.stack(order + [lax.axis_index("z") * 2 + lax.axis_index("yl")]).astype(jnp.int32)
    blocks = travel.reshape(4, 2, 2, ROWS, CH)

    def travel_for(flip_y, flip_c):
        return lax.dynamic_slice(
            blocks, (0, yh ^ flip_y, core ^ flip_c, 0, 0), (4, 1, 1, ROWS, CH)
        ).reshape(4, ROWS, CH).astype(jnp.int16)

    block = (spectra * quality.astype(bf16)).reshape(1, 48, CH)
    parts = [travel_for(flip // 2, flip % 2) for flip in range(4)]
    place, *parts = tie(place, *parts)

    def moved(flip):
        return lax.ppermute(parts[flip], ("yh", "c"), [(i, i ^ flip) for i in range(4)])

    def exchange(values, stage):
        if stage == 0:
            return lax.ppermute(values, "yh", SWAP)
        mask = (1, 8, 4, 2)[stage - 1]
        return lax.ppermute(values, ("z", "yl"), [(i, i ^ mask) for i in range(16)])

    held = block
    other = exchange(held, 0)
    held = join(held, other, other)
    held, *parts = tie(held, *parts)
    far, near, both = moved(2), moved(1), moved(3)
    other = exchange(held, 1)
    rep_own, token = replicas(place, parts[0], held, "own")
    held = join(held, other, token)
    other = exchange(held, 2)
    rep_near, token = replicas(place, near, held, "near")
    held = join(held, other, token)
    other = exchange(held, 3)
    held = join(held, other, token)
    held, far = tie(held, far)
    other = exchange(held, 4)
    held_swapped = lax.ppermute(held, "c", SWAP)
    rep_far, token = replicas(place, far, held, "far")
    other_swapped = lax.ppermute(other, "c", SWAP)
    rep_both, _ = replicas(place, both, other, "both")
    halves = ((held, other, 0), (held_swapped, other_swapped, 0), (held, other, 1), (held_swapped, other_swapped, 1))
    prepared = [prepare(*half, 4 * index) for index, half in enumerate(halves)]
    weights, norms = [w for w, _ in prepared], [n for _, n in prepared]
    reps = (rep_own, rep_near, rep_far, rep_both)
    received = []
    for step, dx in enumerate(STEPS):
        if step == 3:
            norms[0], received[0] = tie(norms[0], received[0])
        beams = beams_block(reps, weights, norms, step)
        if dx:
            received.append(lax.ppermute(beams, "x", [(i, (i + dx) % 4) for i in range(4)]))
    return finish(place, received, beams, norms, float(NF * CH * 16))


def solution(mesh):
    fine = Mesh(mesh.devices.reshape(8, 2, 4, 2, 2), ("z", "yl", "x", "yh", "c"))
    return jax.shard_map(
        per_device,
        mesh=fine,
        in_specs=(
            P(None, None, ("z", "yl"), ("x", "yh", "c")),
            P(("z", "yl"), ("x", "yh", "c")),
            P(("x", "yh", "c")),
        ),
        out_specs=P(None, ("z", "yl", "x", "yh", "c")),
        check_vma=False,
    )
```

```python
import functools

import jax
import jax.numpy as jnp
import numpy as np
from jax import lax
from jax.experimental import pallas as pl
from jax.experimental.pallas import tpu as pltpu
from jax.sharding import Mesh, PartitionSpec as P

NFFT = 2048
lowest_bin = 37
bin_spacing = 29
f32 = jnp.float32
bf16 = jnp.bfloat16

NF = 8
ROWS = 256
CH = 256
COLS = 96
TILE = 32
NORM_ROWS = 16


def series_coefficients():
    nodes = np.cos(np.linspace(0, np.pi, 4002)) / 8
    squares = nodes**2
    angles = 2 * np.pi * nodes
    sine = np.linalg.lstsq(squares[:, None] ** np.arange(4), np.sin(angles) / nodes, rcond=None)[0]
    cosine = np.linalg.lstsq(squares[:, None] ** np.arange(5), np.cos(angles), rcond=None)[0]
    return [np.float32(v) for v in sine], [np.float32(v) for v in cosine]


SINE, COSINE = series_coefficients()


def horner(coefficients, value):
    total = coefficients[-1]
    for coefficient in coefficients[-2::-1]:
        total = coefficient + value * total
    return total


def unit_circle(turns_times, multiple):
    turns = turns_times * np.float32(multiple / NFFT)
    magic = np.float32(1.5 * 2**23)
    part = turns - ((turns + magic) - magic)
    quarter = part * np.float32(0.25)
    square = quarter * quarter
    sine = quarter * horner(SINE, square)
    cosine = horner(COSINE, square)
    for _ in range(2):
        twice = sine + sine
        sine, cosine = twice * cosine, np.float32(1.0) - twice * sine
    return cosine, sine


def replica_tiles(tau):
    delay = tau.astype(f32)
    c0, s0 = unit_circle(delay, lowest_bin)
    cd, sd = unit_circle(delay, bin_spacing)
    cosines = [c0, c0 * cd - s0 * sd]
    sines = [s0, s0 * cd + c0 * sd]
    twice = cd + cd
    for _ in range(2, NF):
        cosines.append(twice * cosines[-1] - cosines[-2])
        sines.append(twice * sines[-1] - sines[-2])
    return cosines, sines


VMEM = pl.BlockSpec(memory_space=pltpu.VMEM)
BY_COLUMNS = (((1,), (1,)), ((), ()))


def product(left, right):
    return lax.dot_general(left, right, BY_COLUMNS, preferred_element_type=f32)


def thirds(values):
    high = values.astype(bf16)
    rest = values - high.astype(f32)
    middle = rest.astype(bf16)
    low = (rest - middle.astype(f32)).astype(bf16)
    return high, middle, low


def exact_product(ones, values):
    high, middle, low = thirds(values)
    return product(ones, high) + (product(ones, middle) + product(ones, low))


def replicas_kernel(place, travel_ref, after_ref, rep_ref, token_ref):
    block = pl.program_id(0)
    token_ref[...] = jnp.zeros_like(token_ref)

    def body(step, carry):
        rows = pl.ds(pl.multiple_of(step * TILE, TILE), TILE)
        for half in range(CH // 128):
            lanes = slice(half * 128, (half + 1) * 128)
            cosines, sines = replica_tiles(travel_ref[0, rows, lanes].astype(jnp.int32))
            for f in range(NF):
                rep_ref[block, f, rows, lanes] = cosines[f].astype(bf16)
                rep_ref[block, f, rows, CH + half * 128 : CH + (half + 1) * 128] = sines[f].astype(bf16)
        return carry

    lax.fori_loop(0, ROWS // TILE, body, 0)


def replicas(place, travel, after, name):
    def index(i, p):
        return (p[i], 0, 0)

    return pl.pallas_call(
        replicas_kernel,
        grid_spec=pltpu.PrefetchScalarGridSpec(
            num_scalar_prefetch=1,
            grid=(4,),
            in_specs=[pl.BlockSpec((1, ROWS, CH), index), VMEM],
            out_specs=[VMEM, VMEM],
        ),
        out_shape=[
            jax.ShapeDtypeStruct((4, NF, ROWS, 2 * CH), bf16),
            jax.ShapeDtypeStruct((8, 128), jnp.int32),
        ],
        cost_estimate=pl.CostEstimate(flops=40_000_000_000, bytes_accessed=1_000_000, transcendentals=0),
        compiler_params=pltpu.CompilerParams(vmem_limit_bytes=4 << 20),
        name=f"replicas_{name}",
    )(place, travel, after)


def join_kernel(*refs):
    *sources, token_ref, out_ref = refs
    rows = sources[0].shape[0]
    for index, source in enumerate(sources):
        out_ref[index * rows : (index + 1) * rows] = source[...]


def join(token, *arrays):
    first = arrays[0]
    return pl.pallas_call(
        join_kernel,
        in_specs=[VMEM] * (len(arrays) + 1),
        out_specs=VMEM,
        out_shape=jax.ShapeDtypeStruct((len(arrays) * first.shape[0],) + first.shape[1:], first.dtype),
        cost_estimate=pl.CostEstimate(flops=0, bytes_accessed=100_000, transcendentals=0),
        compiler_params=pltpu.CompilerParams(vmem_limit_bytes=2 << 20),
        name=f"join_{first.shape[0]}",
    )(*arrays, token)


def beams_kernel(*refs, slot):
    reps, weights, norms, out_ref = refs[0:4], refs[4:8], refs[8:12], refs[12]
    columns = []
    for f in range(NF):
        parts = [product(rep[slot, f], w_ref[f]) for rep, w_ref in zip(reps, weights)]
        columns.append((parts[0] + parts[1]) + (parts[2] + parts[3]))
    out_ref[0:ROWS] = jnp.concatenate(columns, axis=1).astype(out_ref.dtype)
    if out_ref.shape[0] > ROWS:
        out_ref[ROWS : ROWS + NORM_ROWS] = (norms[0][...] + norms[1][...]) + (norms[2][...] + norms[3][...])


def beams_block(reps, weights, norms, step):
    own = STEPS[step] == 0
    rows = ROWS if own else ROWS + NORM_ROWS
    return pl.pallas_call(
        functools.partial(beams_kernel, slot=step),
        in_specs=[VMEM] * 12,
        out_specs=VMEM,
        out_shape=jax.ShapeDtypeStruct((rows, NF * COLS), f32 if own else bf16),
        cost_estimate=pl.CostEstimate(flops=3_000_000_000, bytes_accessed=1_000_000, transcendentals=0),
        compiler_params=pltpu.CompilerParams(vmem_limit_bytes=4 << 20),
        name=f"beams_{step}",
    )(*reps, *weights, *norms)


def prepare_kernel(low_ref, high_ref, w_ref, norm_ref, wide, *, flip, first_row):
    for g in range(16):
        source_ref, class_row = (low_ref, 0) if g < 4 else (high_ref, 8 * (g // 4 - 1))
        for half in range(CH // 128):
            lanes = slice(half * 128, (half + 1) * 128)
            wide[half, g * 48 : (g + 1) * 48, :] = source_ref[class_row + 2 * (g % 4) + flip, :, lanes].astype(f32)
    squares = jnp.zeros((COLS, CH), f32)
    for f in range(NF):
        real, imag = [
            jnp.concatenate(
                [
                    jnp.concatenate(
                        [
                            wide[half, pl.ds(p * 24 + f * 3 + i, 16, stride=48), :]
                            for half in range(CH // 128)
                        ],
                        axis=1,
                    )
                    for i in range(3)
                ],
                axis=0,
            )
            for p in range(2)
        ]
        both = jnp.concatenate([real, imag], axis=0)
        squares = squares + both * both
        w_ref[f, :, 0:CH] = both.astype(bf16)
        w_ref[f, :, CH : 2 * CH] = jnp.concatenate([-imag, real], axis=0).astype(bf16)
    sums = exact_product(jnp.ones((NORM_ROWS, CH), bf16), squares)
    row = lax.broadcasted_iota(jnp.int32, sums.shape, 0) - first_row
    zero = jnp.zeros_like(sums)
    split = zero
    for index, part in enumerate(thirds(sums)):
        split = jnp.where(row == index, part.astype(f32), split)
    norm_ref[...] = jnp.concatenate([split] + [zero] * (NF - 1), axis=1).astype(bf16)


def prepare(low, high, flip, first_row):
    return pl.pallas_call(
        functools.partial(prepare_kernel, flip=flip, first_row=first_row),
        in_specs=[VMEM] * 2,
        out_specs=[VMEM, VMEM],
        scratch_shapes=[pltpu.VMEM((CH // 128, 768, 128), f32)],
        out_shape=[
            jax.ShapeDtypeStruct((NF, COLS, 2 * CH), bf16),
            jax.ShapeDtypeStruct((NORM_ROWS, NF * COLS), bf16),
        ],
        cost_estimate=pl.CostEstimate(flops=1_000_000_000, bytes_accessed=1_000_000, transcendentals=0),
        compiler_params=pltpu.CompilerParams(vmem_limit_bytes=6 << 20),
        name=f"prepare_{first_row}",
    )(low, high)


def column_tables():
    slot = np.arange(NF * COLS) % 48
    source = slot % 16
    step_z = np.array([0, 1, 7, 2])[source // 4]
    return np.stack([step_z, source % 2, source % 4 // 2 * 4, slot // 16]).astype(np.int32)


def finish_kernel(place, *refs, count):
    received, own_ref, norms, table_ref, out_ref = refs[0:3], refs[3], refs[4:8], refs[8], refs[9]
    window = lax.broadcasted_iota(jnp.int32, (48, NF * COLS), 0)
    step_z, flip_yl, flip_z, part = [table_ref[row : row + 1, :] for row in range(4)]
    z, yl = place[4], place[5]
    step_z = step_z + jnp.where(step_z == 2, 4 * (1 - z % 2), 0)
    source = 2 * (((z + step_z) & 7) ^ flip_z) + (yl ^ flip_yl)
    pick = jnp.where(window == 3 * source + part, 1.0, 0.0).astype(bf16)
    beams = own_ref[...]
    norm_rows = sum(ref[...].astype(f32) for ref in norms)
    for ref in received:
        beams = beams + ref[0:ROWS].astype(f32)
        norm_rows = norm_rows + ref[ROWS : ROWS + NORM_ROWS].astype(f32)
    norm_sum = jnp.sum(exact_product(pick, norm_rows), axis=1, keepdims=True)
    window_norm = norm_sum / count + 1e-06
    out_ref[...] = exact_product(pick, beams * beams) / (count * window_norm)


def finish(place, received, own, norms, count):
    return pl.pallas_call(
        functools.partial(finish_kernel, count=count),
        in_specs=[pl.BlockSpec(memory_space=pltpu.SMEM)] + [VMEM] * 9,
        out_specs=VMEM,
        out_shape=jax.ShapeDtypeStruct((48, ROWS), f32),
        compiler_params=pltpu.CompilerParams(vmem_limit_bytes=8 << 20),
        name="finish",
    )(place, *received, own, *norms, jnp.asarray(column_tables()))


STEPS = (2, 1, 3, 0)
SWAP = [(0, 1), (1, 0)]


def tie(*values):
    return lax.optimization_barrier(values)


def per_device(spectra, travel, quality):
    x, yh, core = lax.axis_index("x"), lax.axis_index("yh"), lax.axis_index("c")
    order = [(x + dx) % 4 for dx in STEPS]
    place = jnp.stack(order + [lax.axis_index("z"), lax.axis_index("yl")]).astype(jnp.int32)
    blocks = travel.reshape(4, 2, 2, ROWS, CH)

    def travel_for(flip_y, flip_c):
        return lax.dynamic_slice(
            blocks, (0, yh ^ flip_y, core ^ flip_c, 0, 0), (4, 1, 1, ROWS, CH)
        ).reshape(4, ROWS, CH).astype(jnp.int16)

    block = (spectra * quality.astype(bf16)).reshape(1, 48, CH)
    parts = [travel_for(flip // 2, flip % 2) for flip in range(4)]
    place, *parts = tie(place, *parts)

    def moved(flip):
        return lax.ppermute(parts[flip], ("yh", "c"), [(i, i ^ flip) for i in range(4)])

    def along_z(values, target):
        return lax.ppermute(values, "z", [(i, target(i) % 8) for i in range(8)])

    held = block
    other = lax.ppermute(held, "yh", SWAP)
    held = join(other, held, other)
    held, *parts = tie(held, *parts)
    far, near, both = moved(2), moved(1), moved(3)
    other = lax.ppermute(held, "yl", SWAP)
    rep_own, token = replicas(place, parts[0], held, "own")
    held = join(token, held, other)
    other = along_z(held, lambda i: i ^ 4)
    rep_near, token = replicas(place, near, held, "near")
    held = join(token, held, other)
    two_away = along_z(held, lambda i: i - 2 if i % 2 else i + 2)
    above = along_z(held, lambda i: i - 1)
    below = along_z(held, lambda i: i + 1)
    held_swapped = lax.ppermute(held, "c", SWAP)
    rep_far, token = replicas(place, far, held, "far")
    other = join(token, above, below, two_away)
    other_swapped = lax.ppermute(other, "c", SWAP)
    rep_both, _ = replicas(place, both, other, "both")
    halves = ((held, other, 0), (held_swapped, other_swapped, 0), (held, other, 1), (held_swapped, other_swapped, 1))
    prepared = [prepare(*half, 4 * index) for index, half in enumerate(halves)]
    weights, norms = [w for w, _ in prepared], [n for _, n in prepared]
    reps = (rep_own, rep_near, rep_far, rep_both)
    received = []
    for step, dx in enumerate(STEPS):
        if step == 3:
            norms[0], received[0] = tie(norms[0], received[0])
        beams = beams_block(reps, weights, norms, step)
        if dx:
            received.append(lax.ppermute(beams, "x", [(i, (i + dx) % 4) for i in range(4)]))
    return finish(place, received, beams, norms, float(NF * CH * 16))


def solution(mesh):
    fine = Mesh(mesh.devices.reshape(8, 2, 4, 2, 2), ("z", "yl", "x", "yh", "c"))
    return jax.shard_map(
        per_device,
        mesh=fine,
        in_specs=(
            P(None, None, ("z", "yl"), ("x", "yh", "c")),
            P(("z", "yl"), ("x", "yh", "c")),
            P(("x", "yh", "c")),
        ),
        out_specs=P(None, ("z", "yl", "x", "yh", "c")),
        check_vma=False,
    )
```

```python
import functools

import jax
import jax.numpy as jnp
import numpy as np
from jax import lax
from jax.experimental import pallas as pl
from jax.experimental.pallas import tpu as pltpu
from jax.sharding import Mesh, PartitionSpec as P

NFFT = 2048
lowest_bin = 37
bin_spacing = 29
f32 = jnp.float32
bf16 = jnp.bfloat16

NF = 8
ROWS = 256
CH = 256
COLS = 96
TILE = 32
NORM_ROWS = 16


SINE = [np.float32(1.570796305), np.float32(-0.6459629382), np.float32(0.07967590293), np.float32(-0.004592288967)]
COSINE = [np.float32(0.9999999724), np.float32(-1.233697014), np.float32(0.2535986436), np.float32(-0.02040835128)]


def horner(coefficients, value):
    total = coefficients[-1]
    for coefficient in coefficients[-2::-1]:
        total = coefficient + value * total
    return total


def unit_circle(turns_times, multiple):
    turns = turns_times * np.float32(multiple / NFFT)
    magic = np.float32(1.5 * 2**23)
    part = turns - ((turns + magic) - magic)
    square = part * part
    sine = part * horner(SINE, square)
    cosine = horner(COSINE, square)
    for _ in range(2):
        twice = sine + sine
        sine, cosine = twice * cosine, np.float32(1.0) - twice * sine
    return cosine, sine


def replica_tiles(tau):
    delay = tau.astype(f32)
    c0, s0 = unit_circle(delay, lowest_bin)
    cd, sd = unit_circle(delay, bin_spacing)
    cosines = [c0, c0 * cd - s0 * sd]
    sines = [s0, s0 * cd + c0 * sd]
    twice = cd + cd
    for _ in range(2, NF):
        cosines.append(twice * cosines[-1] - cosines[-2])
        sines.append(twice * sines[-1] - sines[-2])
    return cosines, sines


VMEM = pl.BlockSpec(memory_space=pltpu.VMEM)
BY_COLUMNS = (((1,), (1,)), ((), ()))


def product(left, right):
    return lax.dot_general(left, right, BY_COLUMNS, preferred_element_type=f32)


def eight_bits(values):
    scaled = values * np.float32(65537.0)
    return scaled - (scaled - values)


def thirds(values):
    high = eight_bits(values)
    rest = values - high
    middle = eight_bits(rest)
    return high.astype(bf16), middle.astype(bf16), (rest - middle).astype(bf16)


def exact_product(ones, values):
    high, middle, low = thirds(values)
    return product(ones, high) + (product(ones, middle) + product(ones, low))


def replicas_kernel(place, travel_ref, after_ref, rep_ref, token_ref):
    block = pl.program_id(0)
    token_ref[...] = jnp.zeros_like(token_ref)

    def body(step, carry):
        rows = pl.ds(pl.multiple_of(step * TILE, TILE), TILE)
        for half in range(CH // 128):
            lanes = slice(half * 128, (half + 1) * 128)
            cosines, sines = replica_tiles(travel_ref[0, rows, lanes].astype(jnp.int32))
            for f in range(NF):
                rep_ref[block, f, rows, lanes] = cosines[f].astype(bf16)
                rep_ref[block, f, rows, CH + half * 128 : CH + (half + 1) * 128] = sines[f].astype(bf16)
        return carry

    lax.fori_loop(0, ROWS // TILE, body, 0)


def replicas(place, travel, after, name):
    def index(i, p):
        return (p[i], 0, 0)

    return pl.pallas_call(
        replicas_kernel,
        grid_spec=pltpu.PrefetchScalarGridSpec(
            num_scalar_prefetch=1,
            grid=(4,),
            in_specs=[pl.BlockSpec((1, ROWS, CH), index), VMEM],
            out_specs=[VMEM, VMEM],
        ),
        out_shape=[
            jax.ShapeDtypeStruct((4, NF, ROWS, 2 * CH), bf16),
            jax.ShapeDtypeStruct((8, 128), jnp.int32),
        ],
        cost_estimate=pl.CostEstimate(flops=40_000_000_000, bytes_accessed=1_000_000, transcendentals=0),
        compiler_params=pltpu.CompilerParams(vmem_limit_bytes=4 << 20),
        name=f"replicas_{name}",
    )(place, travel, after)


def join_kernel(*refs):
    *sources, token_ref, out_ref = refs
    rows = sources[0].shape[0]
    for index, source in enumerate(sources):
        out_ref[index * rows : (index + 1) * rows] = source[...]


def join(token, *arrays):
    first = arrays[0]
    return pl.pallas_call(
        join_kernel,
        in_specs=[VMEM] * (len(arrays) + 1),
        out_specs=VMEM,
        out_shape=jax.ShapeDtypeStruct((len(arrays) * first.shape[0],) + first.shape[1:], first.dtype),
        cost_estimate=pl.CostEstimate(flops=0, bytes_accessed=100_000, transcendentals=0),
        compiler_params=pltpu.CompilerParams(vmem_limit_bytes=2 << 20),
        name=f"join_{first.shape[0]}",
    )(*arrays, token)


def beams_kernel(*refs, slot):
    reps, weights, norms, out_ref = refs[0:4], refs[4:8], refs[8:12], refs[12]
    columns = []
    for f in range(NF):
        parts = [product(rep[slot, f], w_ref[f]) for rep, w_ref in zip(reps, weights)]
        columns.append((parts[0] + parts[1]) + (parts[2] + parts[3]))
    out_ref[0:ROWS] = jnp.concatenate(columns, axis=1).astype(out_ref.dtype)
    if out_ref.shape[0] > ROWS:
        out_ref[ROWS : ROWS + NORM_ROWS] = (norms[0][...] + norms[1][...]) + (norms[2][...] + norms[3][...])


def beams_block(reps, weights, norms, step):
    own = STEPS[step] == 0
    rows = ROWS if own else ROWS + NORM_ROWS
    return pl.pallas_call(
        functools.partial(beams_kernel, slot=step),
        in_specs=[VMEM] * 12,
        out_specs=VMEM,
        out_shape=jax.ShapeDtypeStruct((rows, NF * COLS), f32 if own else bf16),
        cost_estimate=pl.CostEstimate(flops=3_000_000_000, bytes_accessed=1_000_000, transcendentals=0),
        compiler_params=pltpu.CompilerParams(vmem_limit_bytes=4 << 20),
        name=f"beams_{step}",
    )(*reps, *weights, *norms)


def prepare_kernel(source_ref, w_ref, norm_ref, wide, *, flip, first_row):
    for g in range(16):
        class_row = 8 * (g // 4)
        for half in range(CH // 128):
            lanes = slice(half * 128, (half + 1) * 128)
            wide[half, g * 48 : (g + 1) * 48, :] = source_ref[class_row + 2 * (g % 4) + flip, :, lanes].astype(f32)
    squares = jnp.zeros((COLS, CH), f32)
    for f in range(NF):
        real, imag = [
            jnp.concatenate(
                [
                    jnp.concatenate(
                        [
                            wide[half, pl.ds(p * 24 + f * 3 + i, 16, stride=48), :]
                            for half in range(CH // 128)
                        ],
                        axis=1,
                    )
                    for i in range(3)
                ],
                axis=0,
            )
            for p in range(2)
        ]
        both = jnp.concatenate([real, imag], axis=0)
        squares = squares + both * both
        w_ref[f, :, 0:CH] = both.astype(bf16)
        w_ref[f, :, CH : 2 * CH] = jnp.concatenate([-imag, real], axis=0).astype(bf16)
    sums = exact_product(jnp.ones((NORM_ROWS, CH), bf16), squares)
    row = lax.broadcasted_iota(jnp.int32, sums.shape, 0) - first_row
    zero = jnp.zeros_like(sums)
    split = zero
    for index, part in enumerate(thirds(sums)):
        split = jnp.where(row == index, part.astype(f32), split)
    norm_ref[...] = jnp.concatenate([split] + [zero] * (NF - 1), axis=1).astype(bf16)


def prepare(source, flip, first_row):
    return pl.pallas_call(
        functools.partial(prepare_kernel, flip=flip, first_row=first_row),
        in_specs=[VMEM],
        out_specs=[VMEM, VMEM],
        scratch_shapes=[pltpu.VMEM((CH // 128, 768, 128), f32)],
        out_shape=[
            jax.ShapeDtypeStruct((NF, COLS, 2 * CH), bf16),
            jax.ShapeDtypeStruct((NORM_ROWS, NF * COLS), bf16),
        ],
        cost_estimate=pl.CostEstimate(flops=1_000_000_000, bytes_accessed=1_000_000, transcendentals=0),
        compiler_params=pltpu.CompilerParams(vmem_limit_bytes=6 << 20),
        name=f"prepare_{first_row}",
    )(source)


def column_tables():
    slot = np.arange(NF * COLS) % 48
    source = slot % 16
    step_z = np.array([0, 1, 7, 2])[source // 4]
    return np.stack([step_z, source % 2, source % 4 // 2 * 4, slot // 16]).astype(np.int32)


def finish_kernel(place, *refs, count):
    received, own_ref, norms, table_ref, out_ref = refs[0:3], refs[3], refs[4:8], refs[8], refs[9]
    window = lax.broadcasted_iota(jnp.int32, (48, NF * COLS), 0)
    step_z, flip_yl, flip_z, part = [table_ref[row : row + 1, :] for row in range(4)]
    z, yl = place[4], place[5]
    step_z = step_z + jnp.where(step_z == 2, 4 * (1 - z % 2), 0)
    source = 2 * (((z + step_z) & 7) ^ flip_z) + (yl ^ flip_yl)
    pick = jnp.where(window == 3 * source + part, 1.0, 0.0).astype(bf16)
    beams = own_ref[...]
    norm_rows = sum(ref[...].astype(f32) for ref in norms)
    for ref in received:
        beams = beams + ref[0:ROWS].astype(f32)
        norm_rows = norm_rows + ref[ROWS : ROWS + NORM_ROWS].astype(f32)
    norm_sum = jnp.sum(exact_product(pick, norm_rows), axis=1, keepdims=True)
    window_norm = norm_sum / count + 1e-06
    out_ref[...] = exact_product(pick, beams * beams) / (count * window_norm)


def finish(place, received, own, norms, count):
    return pl.pallas_call(
        functools.partial(finish_kernel, count=count),
        in_specs=[pl.BlockSpec(memory_space=pltpu.SMEM)] + [VMEM] * 9,
        out_specs=VMEM,
        out_shape=jax.ShapeDtypeStruct((48, ROWS), f32),
        compiler_params=pltpu.CompilerParams(vmem_limit_bytes=8 << 20),
        name="finish",
    )(place, *received, own, *norms, jnp.asarray(column_tables()))


STEPS = (2, 1, 3, 0)
SWAP = [(0, 1), (1, 0)]


def tie(*values):
    return lax.optimization_barrier(values)


def per_device(spectra, travel, quality):
    x, yh, core = lax.axis_index("x"), lax.axis_index("yh"), lax.axis_index("c")
    order = [(x + dx) % 4 for dx in STEPS]
    place = jnp.stack(order + [lax.axis_index("z"), lax.axis_index("yl")]).astype(jnp.int32)
    blocks = travel.reshape(4, 2, 2, ROWS, CH)

    def travel_for(flip_y, flip_c):
        return lax.dynamic_slice(
            blocks, (0, yh ^ flip_y, core ^ flip_c, 0, 0), (4, 1, 1, ROWS, CH)
        ).reshape(4, ROWS, CH).astype(jnp.int16)

    block = (spectra * quality.astype(bf16)).reshape(1, 48, CH)
    parts = [travel_for(flip // 2, flip % 2) for flip in range(4)]
    place, *parts = tie(place, *parts)

    def moved(flip):
        return lax.ppermute(parts[flip], ("yh", "c"), [(i, i ^ flip) for i in range(4)])

    def along_z(values, target):
        return lax.ppermute(values, "z", [(i, target(i) % 8) for i in range(8)])

    held = block
    other = lax.ppermute(held, "yh", SWAP)
    held = join(other, held, other)
    held, *parts = tie(held, *parts)
    far, near, both = moved(2), moved(1), moved(3)
    other = lax.ppermute(held, "yl", SWAP)
    rep_own, token = replicas(place, parts[0], held, "own")
    held = join(token, held, other)
    other = along_z(held, lambda i: i ^ 4)
    rep_near, token = replicas(place, near, held, "near")
    held = join(token, held, other)
    two_away = along_z(held, lambda i: i - 2 if i % 2 else i + 2)
    above = along_z(held, lambda i: i - 1)
    below = along_z(held, lambda i: i + 1)
    rep_far, token = replicas(place, far, held, "far")
    held = join(token, held, above, below, two_away)
    swapped = lax.ppermute(held, "c", SWAP)
    rep_both, _ = replicas(place, both, held, "both")
    halves = ((held, 0), (swapped, 0), (held, 1), (swapped, 1))
    prepared = [prepare(*half, 4 * index) for index, half in enumerate(halves)]
    weights, norms = [w for w, _ in prepared], [n for _, n in prepared]
    reps = (rep_own, rep_near, rep_far, rep_both)
    received = []
    for step, dx in enumerate(STEPS):
        if step == 3:
            norms[0], received[0] = tie(norms[0], received[0])
        beams = beams_block(reps, weights, norms, step)
        if dx:
            received.append(lax.ppermute(beams, "x", [(i, (i + dx) % 4) for i in range(4)]))
    return finish(place, received, beams, norms, float(NF * CH * 16))


def solution(mesh):
    fine = Mesh(mesh.devices.reshape(8, 2, 4, 2, 2), ("z", "yl", "x", "yh", "c"))
    return jax.shard_map(
        per_device,
        mesh=fine,
        in_specs=(
            P(None, None, ("z", "yl"), ("x", "yh", "c")),
            P(("z", "yl"), ("x", "yh", "c")),
            P(("x", "yh", "c")),
        ),
        out_specs=P(None, ("z", "yl", "x", "yh", "c")),
        check_vma=False,
    )
```

```python
import functools

import jax
import jax.numpy as jnp
import numpy as np
from jax import lax
from jax.experimental import pallas as pl
from jax.experimental.pallas import tpu as pltpu
from jax.sharding import Mesh, PartitionSpec as P

NFFT = 2048
lowest_bin = 37
bin_spacing = 29
f32 = jnp.float32
bf16 = jnp.bfloat16

NF = 8
ROWS = 256
CH = 256
COLS = 96
TILE = 32
NORM_ROWS = 8


SINE = [np.float32(1.570796305), np.float32(-0.6459629382), np.float32(0.07967590293), np.float32(-0.004592288967)]
COSINE = [np.float32(0.9999999724), np.float32(-1.233697014), np.float32(0.2535986436), np.float32(-0.02040835128)]


def horner(coefficients, value):
    total = coefficients[-1]
    for coefficient in coefficients[-2::-1]:
        total = coefficient + value * total
    return total


def unit_circle(turns_times, multiple):
    turns = turns_times * np.float32(multiple / NFFT)
    magic = np.float32(1.5 * 2**23)
    part = turns - ((turns + magic) - magic)
    square = part * part
    sine = part * horner(SINE, square)
    cosine = horner(COSINE, square)
    for _ in range(2):
        twice = sine + sine
        sine, cosine = twice * cosine, np.float32(1.0) - twice * sine
    return cosine, sine


def replica_tiles(tau):
    delay = tau.astype(f32)
    c0, s0 = unit_circle(delay, lowest_bin)
    cd, sd = unit_circle(delay, bin_spacing)
    cosines = [c0, c0 * cd - s0 * sd]
    sines = [s0, s0 * cd + c0 * sd]
    twice = cd + cd
    for _ in range(2, NF):
        cosines.append(twice * cosines[-1] - cosines[-2])
        sines.append(twice * sines[-1] - sines[-2])
    return cosines, sines


VMEM = pl.BlockSpec(memory_space=pltpu.VMEM)
BY_COLUMNS = (((1,), (1,)), ((), ()))


def product(left, right):
    return lax.dot_general(left, right, BY_COLUMNS, preferred_element_type=f32)


def eight_bits(values):
    scaled = values * np.float32(65537.0)
    return scaled - (scaled - values)


def thirds(values):
    high = eight_bits(values)
    rest = values - high
    middle = eight_bits(rest)
    return high.astype(bf16), middle.astype(bf16), (rest - middle).astype(bf16)


def exact_product(ones, values):
    high, middle, low = thirds(values)
    return product(ones, high) + (product(ones, middle) + product(ones, low))


def replicas_kernel(place, travel_ref, after_ref, rep_ref, token_ref):
    block = pl.program_id(0)
    token_ref[...] = jnp.zeros_like(token_ref)

    def body(step, carry):
        rows = pl.ds(pl.multiple_of(step * TILE, TILE), TILE)
        for half in range(CH // 128):
            lanes = slice(half * 128, (half + 1) * 128)
            cosines, sines = replica_tiles(travel_ref[0, rows, lanes].astype(jnp.int32))
            for f in range(NF):
                rep_ref[block, f, rows, lanes] = cosines[f].astype(bf16)
                rep_ref[block, f, rows, CH + half * 128 : CH + (half + 1) * 128] = sines[f].astype(bf16)
        return carry

    lax.fori_loop(0, ROWS // TILE, body, 0)


def replicas(place, travel, after, name):
    def index(i, p):
        return (p[i], 0, 0)

    return pl.pallas_call(
        replicas_kernel,
        grid_spec=pltpu.PrefetchScalarGridSpec(
            num_scalar_prefetch=1,
            grid=(4,),
            in_specs=[pl.BlockSpec((1, ROWS, CH), index), VMEM],
            out_specs=[VMEM, VMEM],
        ),
        out_shape=[
            jax.ShapeDtypeStruct((4, NF, ROWS, 2 * CH), bf16),
            jax.ShapeDtypeStruct((8, 128), jnp.int32),
        ],
        cost_estimate=pl.CostEstimate(flops=40_000_000_000, bytes_accessed=1_000_000, transcendentals=0),
        compiler_params=pltpu.CompilerParams(vmem_limit_bytes=4 << 20),
        name=f"replicas_{name}",
    )(place, travel, after)


def join_kernel(*refs):
    *sources, token_ref, out_ref = refs
    rows = sources[0].shape[0]
    for index, source in enumerate(sources):
        out_ref[index * rows : (index + 1) * rows] = source[...]


def join(token, *arrays):
    first = arrays[0]
    return pl.pallas_call(
        join_kernel,
        in_specs=[VMEM] * (len(arrays) + 1),
        out_specs=VMEM,
        out_shape=jax.ShapeDtypeStruct((len(arrays) * first.shape[0],) + first.shape[1:], first.dtype),
        cost_estimate=pl.CostEstimate(flops=0, bytes_accessed=100_000, transcendentals=0),
        compiler_params=pltpu.CompilerParams(vmem_limit_bytes=2 << 20),
        name=f"join_{first.shape[0]}",
    )(*arrays, token)


def beams_kernel(*refs, slot):
    reps, weights, norms, out_ref = refs[0:4], refs[4:8], refs[8:12], refs[12]
    columns = []
    for f in range(NF):
        parts = [product(rep[slot, f], w_ref[f]) for rep, w_ref in zip(reps, weights)]
        columns.append((parts[0] + parts[1]) + (parts[2] + parts[3]))
    out_ref[0:ROWS] = jnp.concatenate(columns, axis=1).astype(out_ref.dtype)
    if out_ref.shape[0] > ROWS:
        out_ref[ROWS : ROWS + NORM_ROWS] = (norms[0][...] + norms[1][...]) + (norms[2][...] + norms[3][...])


def beams_block(reps, weights, norms, step):
    own = STEPS[step] == 0
    rows = ROWS if own else ROWS + NORM_ROWS
    return pl.pallas_call(
        functools.partial(beams_kernel, slot=step),
        in_specs=[VMEM] * 12,
        out_specs=VMEM,
        out_shape=jax.ShapeDtypeStruct((rows, NF * COLS), f32 if own else bf16),
        cost_estimate=pl.CostEstimate(flops=3_000_000_000, bytes_accessed=1_000_000, transcendentals=0),
        compiler_params=pltpu.CompilerParams(vmem_limit_bytes=4 << 20),
        name=f"beams_{step}",
    )(*reps, *weights, *norms)


def prepare_kernel(source_ref, w_ref, norm_ref, wide, *, flip, first_row):
    for g in range(16):
        class_row = 8 * (g // 4)
        for half in range(CH // 128):
            lanes = slice(half * 128, (half + 1) * 128)
            wide[half, g * 48 : (g + 1) * 48, :] = source_ref[class_row + 2 * (g % 4) + flip, :, lanes].astype(f32)
    squares = jnp.zeros((COLS, CH), f32)
    for f in range(NF):
        real, imag = [
            jnp.concatenate(
                [
                    jnp.concatenate(
                        [
                            wide[half, pl.ds(p * 24 + f * 3 + i, 16, stride=48), :]
                            for half in range(CH // 128)
                        ],
                        axis=1,
                    )
                    for i in range(3)
                ],
                axis=0,
            )
            for p in range(2)
        ]
        both = jnp.concatenate([real, imag], axis=0)
        squares = squares + both * both
        w_ref[f, :, 0:CH] = both.astype(bf16)
        w_ref[f, :, CH : 2 * CH] = jnp.concatenate([-imag, real], axis=0).astype(bf16)
    sums = exact_product(jnp.ones((NORM_ROWS, CH), bf16), squares)
    row = lax.broadcasted_iota(jnp.int32, sums.shape, 0) - first_row
    zero = jnp.zeros_like(sums)
    split = zero
    for index, part in enumerate(thirds(sums)[:2]):
        split = jnp.where(row == index, part.astype(f32), split)
    norm_ref[...] = jnp.concatenate([split] + [zero] * (NF - 1), axis=1).astype(bf16)


def prepare(source, flip, first_row):
    return pl.pallas_call(
        functools.partial(prepare_kernel, flip=flip, first_row=first_row),
        in_specs=[VMEM],
        out_specs=[VMEM, VMEM],
        scratch_shapes=[pltpu.VMEM((CH // 128, 768, 128), f32)],
        out_shape=[
            jax.ShapeDtypeStruct((NF, COLS, 2 * CH), bf16),
            jax.ShapeDtypeStruct((NORM_ROWS, NF * COLS), bf16),
        ],
        cost_estimate=pl.CostEstimate(flops=1_000_000_000, bytes_accessed=1_000_000, transcendentals=0),
        compiler_params=pltpu.CompilerParams(vmem_limit_bytes=6 << 20),
        name=f"prepare_{first_row}",
    )(source)


def column_tables():
    slot = np.arange(NF * COLS) % 48
    source = slot % 16
    step_z = np.array([0, 1, 7, 2])[source // 4]
    return np.stack([step_z, source % 2, source % 4 // 2 * 4, slot // 16]).astype(np.int32)


def finish_kernel(place, *refs, count):
    received, own_ref, norms, table_ref, out_ref = refs[0:3], refs[3], refs[4:8], refs[8], refs[9]
    window = lax.broadcasted_iota(jnp.int32, (48, NF * COLS), 0)
    step_z, flip_yl, flip_z, part = [table_ref[row : row + 1, :] for row in range(4)]
    z, yl = place[4], place[5]
    step_z = step_z + jnp.where(step_z == 2, 4 * (1 - z % 2), 0)
    source = 2 * (((z + step_z) & 7) ^ flip_z) + (yl ^ flip_yl)
    pick = jnp.where(window == 3 * source + part, 1.0, 0.0).astype(bf16)
    beams = own_ref[...]
    norm_rows = sum(ref[...].astype(f32) for ref in norms)
    for ref in received:
        beams = beams + ref[0:ROWS].astype(f32)
        norm_rows = norm_rows + ref[ROWS : ROWS + NORM_ROWS].astype(f32)
    norm_sum = jnp.sum(exact_product(pick, norm_rows), axis=1, keepdims=True)
    window_norm = norm_sum / count + 1e-06
    out_ref[...] = exact_product(pick, beams * beams) / (count * window_norm)


def finish(place, received, own, norms, count):
    return pl.pallas_call(
        functools.partial(finish_kernel, count=count),
        in_specs=[pl.BlockSpec(memory_space=pltpu.SMEM)] + [VMEM] * 9,
        out_specs=VMEM,
        out_shape=jax.ShapeDtypeStruct((48, ROWS), f32),
        compiler_params=pltpu.CompilerParams(vmem_limit_bytes=8 << 20),
        name="finish",
    )(place, *received, own, *norms, jnp.asarray(column_tables()))


STEPS = (2, 1, 3, 0)
SWAP = [(0, 1), (1, 0)]


def tie(*values):
    return lax.optimization_barrier(values)


def per_device(spectra, travel, quality):
    x, yh, core = lax.axis_index("x"), lax.axis_index("yh"), lax.axis_index("c")
    order = [(x + dx) % 4 for dx in STEPS]
    place = jnp.stack(order + [lax.axis_index("z"), lax.axis_index("yl")]).astype(jnp.int32)
    blocks = travel.reshape(4, 2, 2, ROWS, CH)

    def travel_for(flip_y, flip_c):
        return lax.dynamic_slice(
            blocks, (0, yh ^ flip_y, core ^ flip_c, 0, 0), (4, 1, 1, ROWS, CH)
        ).reshape(4, ROWS, CH).astype(jnp.int16)

    block = (spectra * quality.astype(bf16)).reshape(1, 48, CH)
    parts = [travel_for(flip // 2, flip % 2) for flip in range(4)]
    place, *parts = tie(place, *parts)

    def moved(flip):
        return lax.ppermute(parts[flip], ("yh", "c"), [(i, i ^ flip) for i in range(4)])

    def along_z(values, target):
        return lax.ppermute(values, "z", [(i, target(i) % 8) for i in range(8)])

    held = block
    other = lax.ppermute(held, "yh", SWAP)
    held = join(other, held, other)
    held, *parts = tie(held, *parts)
    far, near, both = moved(2), moved(1), moved(3)
    other = lax.ppermute(held, "yl", SWAP)
    held = join(other, held, other)
    other = along_z(held, lambda i: i ^ 4)
    rep_own, token = replicas(place, parts[0], held, "own")
    rep_near, token = replicas(place, near, token, "near")
    held = join(token, held, other)
    two_away = along_z(held, lambda i: i - 2 if i % 2 else i + 2)
    above = along_z(held, lambda i: i - 1)
    below = along_z(held, lambda i: i + 1)
    rep_far, token = replicas(place, far, held, "far")
    held = join(token, held, above, below, two_away)
    swapped = lax.ppermute(held, "c", SWAP)
    rep_both, _ = replicas(place, both, held, "both")
    halves = ((held, 0), (swapped, 0), (held, 1), (swapped, 1))
    prepared = [prepare(*half, 2 * index) for index, half in enumerate(halves)]
    weights, norms = [w for w, _ in prepared], [n for _, n in prepared]
    reps = (rep_own, rep_near, rep_far, rep_both)
    received = []
    for step, dx in enumerate(STEPS):
        if step == 3:
            norms[0], received[0] = tie(norms[0], received[0])
        beams = beams_block(reps, weights, norms, step)
        if dx:
            received.append(lax.ppermute(beams, "x", [(i, (i + dx) % 4) for i in range(4)]))
    return finish(place, received, beams, norms, float(NF * CH * 16))


def solution(mesh):
    fine = Mesh(mesh.devices.reshape(8, 2, 4, 2, 2), ("z", "yl", "x", "yh", "c"))
    return jax.shard_map(
        per_device,
        mesh=fine,
        in_specs=(
            P(None, None, ("z", "yl"), ("x", "yh", "c")),
            P(("z", "yl"), ("x", "yh", "c")),
            P(("x", "yh", "c")),
        ),
        out_specs=P(None, ("z", "yl", "x", "yh", "c")),
        check_vma=False,
    )
```

```python
import functools

import jax
import jax.numpy as jnp
import numpy as np
from jax import lax
from jax.experimental import pallas as pl
from jax.experimental.pallas import tpu as pltpu
from jax.sharding import Mesh, PartitionSpec as P

NFFT = 2048
lowest_bin = 37
bin_spacing = 29
f32 = jnp.float32
bf16 = jnp.bfloat16

NF = 8
ROWS = 256
CH = 256
COLS = 96
TILE = 32
NORM_ROWS = 8


SINE = [np.float32(1.570796305), np.float32(-0.6459629382), np.float32(0.07967590293), np.float32(-0.004592288967)]
COSINE = [np.float32(0.9999999724), np.float32(-1.233697014), np.float32(0.2535986436), np.float32(-0.02040835128)]


def horner(coefficients, value):
    total = coefficients[-1]
    for coefficient in coefficients[-2::-1]:
        total = coefficient + value * total
    return total


def unit_circle(turns_times, multiple):
    turns = turns_times * np.float32(multiple / NFFT)
    magic = np.float32(1.5 * 2**23)
    part = turns - ((turns + magic) - magic)
    square = part * part
    sine = part * horner(SINE, square)
    cosine = horner(COSINE, square)
    for _ in range(2):
        twice = sine + sine
        sine, cosine = twice * cosine, np.float32(1.0) - twice * sine
    return cosine, sine


def replica_tiles(tau):
    delay = tau.astype(f32)
    c0, s0 = unit_circle(delay, lowest_bin)
    cd, sd = unit_circle(delay, bin_spacing)
    cosines = [c0, c0 * cd - s0 * sd]
    sines = [s0, s0 * cd + c0 * sd]
    twice = cd + cd
    for _ in range(2, NF):
        cosines.append(twice * cosines[-1] - cosines[-2])
        sines.append(twice * sines[-1] - sines[-2])
    return cosines, sines


VMEM = pl.BlockSpec(memory_space=pltpu.VMEM)
BY_COLUMNS = (((1,), (1,)), ((), ()))


def product(left, right):
    return lax.dot_general(left, right, BY_COLUMNS, preferred_element_type=f32)


def eight_bits(values):
    scaled = values * np.float32(65537.0)
    return scaled - (scaled - values)


def thirds(values):
    high = eight_bits(values)
    rest = values - high
    middle = eight_bits(rest)
    return high.astype(bf16), middle.astype(bf16), (rest - middle).astype(bf16)


def exact_product(ones, values):
    high, middle, low = thirds(values)
    return product(ones, high) + (product(ones, middle) + product(ones, low))


def replicas_kernel(place, travel_ref, after_ref, rep_ref, token_ref):
    block = pl.program_id(0)
    token_ref[...] = jnp.zeros_like(token_ref)

    def body(step, carry):
        rows = pl.ds(pl.multiple_of(step * TILE, TILE), TILE)
        for half in range(CH // 128):
            lanes = slice(half * 128, (half + 1) * 128)
            cosines, sines = replica_tiles(travel_ref[0, rows, lanes].astype(jnp.int32))
            for f in range(NF):
                rep_ref[block, f, rows, lanes] = cosines[f].astype(bf16)
                rep_ref[block, f, rows, CH + half * 128 : CH + (half + 1) * 128] = sines[f].astype(bf16)
        return carry

    lax.fori_loop(0, ROWS // TILE, body, 0)


def replicas(place, travel, after, name, slots=(0, 4)):
    first, stop = slots

    def index(i, p):
        return (p[first + i], 0, 0)

    return pl.pallas_call(
        replicas_kernel,
        grid_spec=pltpu.PrefetchScalarGridSpec(
            num_scalar_prefetch=1,
            grid=(stop - first,),
            in_specs=[pl.BlockSpec((1, ROWS, CH), index), VMEM],
            out_specs=[VMEM, VMEM],
        ),
        out_shape=[
            jax.ShapeDtypeStruct((stop - first, NF, ROWS, 2 * CH), bf16),
            jax.ShapeDtypeStruct((8, 128), jnp.int32),
        ],
        cost_estimate=pl.CostEstimate(flops=40_000_000_000, bytes_accessed=1_000_000, transcendentals=0),
        compiler_params=pltpu.CompilerParams(vmem_limit_bytes=4 << 20),
        name=f"replicas_{name}",
    )(place, travel, after)


def join_kernel(*refs):
    *sources, token_ref, out_ref = refs
    rows = sources[0].shape[0]
    for index, source in enumerate(sources):
        out_ref[index * rows : (index + 1) * rows] = source[...]


def join(token, *arrays):
    first = arrays[0]
    return pl.pallas_call(
        join_kernel,
        in_specs=[VMEM] * (len(arrays) + 1),
        out_specs=VMEM,
        out_shape=jax.ShapeDtypeStruct((len(arrays) * first.shape[0],) + first.shape[1:], first.dtype),
        cost_estimate=pl.CostEstimate(flops=0, bytes_accessed=100_000, transcendentals=0),
        compiler_params=pltpu.CompilerParams(vmem_limit_bytes=2 << 20),
        name=f"join_{first.shape[0]}",
    )(*arrays, token)


def beams_kernel(*refs, slots):
    reps, weights, norms, out_ref = refs[0:4], refs[4:8], refs[8:12], refs[12]
    columns = []
    for f in range(NF):
        parts = [product(rep[slot, f], w_ref[f]) for rep, slot, w_ref in zip(reps, slots, weights)]
        columns.append((parts[0] + parts[1]) + (parts[2] + parts[3]))
    out_ref[0:ROWS] = jnp.concatenate(columns, axis=1).astype(out_ref.dtype)
    if out_ref.shape[0] > ROWS:
        out_ref[ROWS : ROWS + NORM_ROWS] = (norms[0][...] + norms[1][...]) + (norms[2][...] + norms[3][...])


def beams_block(reps, slots, weights, norms, step):
    own = STEPS[step] == 0
    rows = ROWS if own else ROWS + NORM_ROWS
    return pl.pallas_call(
        functools.partial(beams_kernel, slots=slots),
        in_specs=[VMEM] * 12,
        out_specs=VMEM,
        out_shape=jax.ShapeDtypeStruct((rows, NF * COLS), f32 if own else bf16),
        cost_estimate=pl.CostEstimate(flops=3_000_000_000, bytes_accessed=1_000_000, transcendentals=0),
        compiler_params=pltpu.CompilerParams(vmem_limit_bytes=4 << 20),
        name=f"beams_{step}",
    )(*reps, *weights, *norms)


def prepare_kernel(source_ref, w_ref, norm_ref, wide, *, flip, first_row):
    for g in range(16):
        class_row = 8 * (g // 4)
        for half in range(CH // 128):
            lanes = slice(half * 128, (half + 1) * 128)
            wide[half, g * 48 : (g + 1) * 48, :] = source_ref[class_row + 2 * (g % 4) + flip, :, lanes].astype(f32)
    squares = jnp.zeros((COLS, CH), f32)
    for f in range(NF):
        real, imag = [
            jnp.concatenate(
                [
                    jnp.concatenate(
                        [
                            wide[half, pl.ds(p * 24 + f * 3 + i, 16, stride=48), :]
                            for half in range(CH // 128)
                        ],
                        axis=1,
                    )
                    for i in range(3)
                ],
                axis=0,
            )
            for p in range(2)
        ]
        both = jnp.concatenate([real, imag], axis=0)
        squares = squares + both * both
        w_ref[f, :, 0:CH] = both.astype(bf16)
        w_ref[f, :, CH : 2 * CH] = jnp.concatenate([-imag, real], axis=0).astype(bf16)
    sums = exact_product(jnp.ones((NORM_ROWS, CH), bf16), squares)
    row = lax.broadcasted_iota(jnp.int32, sums.shape, 0) - first_row
    zero = jnp.zeros_like(sums)
    split = zero
    for index, part in enumerate(thirds(sums)[:2]):
        split = jnp.where(row == index, part.astype(f32), split)
    norm_ref[...] = jnp.concatenate([split] + [zero] * (NF - 1), axis=1).astype(bf16)


def prepare(source, flip, first_row):
    return pl.pallas_call(
        functools.partial(prepare_kernel, flip=flip, first_row=first_row),
        in_specs=[VMEM],
        out_specs=[VMEM, VMEM],
        scratch_shapes=[pltpu.VMEM((CH // 128, 768, 128), f32)],
        out_shape=[
            jax.ShapeDtypeStruct((NF, COLS, 2 * CH), bf16),
            jax.ShapeDtypeStruct((NORM_ROWS, NF * COLS), bf16),
        ],
        cost_estimate=pl.CostEstimate(flops=1_000_000_000, bytes_accessed=1_000_000, transcendentals=0),
        compiler_params=pltpu.CompilerParams(vmem_limit_bytes=6 << 20),
        name=f"prepare_{first_row}",
    )(source)


def column_tables():
    slot = np.arange(NF * COLS) % 48
    source = slot % 16
    step_z = np.array([0, 1, 7, 2])[source // 4]
    return np.stack([step_z, source % 2, source % 4 // 2 * 4, slot // 16]).astype(np.int32)


def finish_kernel(place, *refs, count):
    received, own_ref, norms, table_ref, out_ref = refs[0:3], refs[3], refs[4:8], refs[8], refs[9]
    window = lax.broadcasted_iota(jnp.int32, (48, NF * COLS), 0)
    step_z, flip_yl, flip_z, part = [table_ref[row : row + 1, :] for row in range(4)]
    z, yl = place[4], place[5]
    step_z = step_z + jnp.where(step_z == 2, 4 * (1 - z % 2), 0)
    source = 2 * (((z + step_z) & 7) ^ flip_z) + (yl ^ flip_yl)
    pick = jnp.where(window == 3 * source + part, 1.0, 0.0).astype(bf16)
    beams = own_ref[...]
    norm_rows = sum(ref[...].astype(f32) for ref in norms)
    for ref in received:
        beams = beams + ref[0:ROWS].astype(f32)
        norm_rows = norm_rows + ref[ROWS : ROWS + NORM_ROWS].astype(f32)
    norm_sum = jnp.sum(exact_product(pick, norm_rows), axis=1, keepdims=True)
    window_norm = norm_sum / count + 1e-06
    out_ref[...] = exact_product(pick, beams * beams) / (count * window_norm)


def finish(place, received, own, norms, count):
    return pl.pallas_call(
        functools.partial(finish_kernel, count=count),
        in_specs=[pl.BlockSpec(memory_space=pltpu.SMEM)] + [VMEM] * 9,
        out_specs=VMEM,
        out_shape=jax.ShapeDtypeStruct((48, ROWS), f32),
        compiler_params=pltpu.CompilerParams(vmem_limit_bytes=8 << 20),
        name="finish",
    )(place, *received, own, *norms, jnp.asarray(column_tables()))


STEPS = (2, 1, 3, 0)
SWAP = [(0, 1), (1, 0)]


def tie(*values):
    return lax.optimization_barrier(values)


def per_device(spectra, travel, quality):
    x, yh, core = lax.axis_index("x"), lax.axis_index("yh"), lax.axis_index("c")
    order = [(x + dx) % 4 for dx in STEPS]
    place = jnp.stack(order + [lax.axis_index("z"), lax.axis_index("yl")]).astype(jnp.int32)
    blocks = travel.reshape(4, 2, 2, ROWS, CH)

    def travel_for(flip_y, flip_c):
        return lax.dynamic_slice(
            blocks, (0, yh ^ flip_y, core ^ flip_c, 0, 0), (4, 1, 1, ROWS, CH)
        ).reshape(4, ROWS, CH).astype(jnp.int16)

    block = (spectra * quality.astype(bf16)).reshape(1, 48, CH)
    parts = [travel_for(flip // 2, flip % 2) for flip in range(4)]
    place, *parts = tie(place, *parts)

    def moved(flip):
        return lax.ppermute(parts[flip], ("yh", "c"), [(i, i ^ flip) for i in range(4)])

    def along_z(values, target):
        return lax.ppermute(values, "z", [(i, target(i) % 8) for i in range(8)])

    held = block
    other = lax.ppermute(held, "yh", SWAP)
    held = join(other, held, other)
    held, *parts = tie(held, *parts)
    far, near, both = moved(2), moved(1), moved(3)
    other = lax.ppermute(held, "yl", SWAP)
    held = join(other, held, other)
    other = along_z(held, lambda i: i ^ 4)
    rep_own, token = replicas(place, parts[0], held, "own")
    rep_near, token = replicas(place, near, token, "near")
    held = join(token, held, other)
    two_away = along_z(held, lambda i: i - 2 if i % 2 else i + 2)
    above = along_z(held, lambda i: i - 1)
    below = along_z(held, lambda i: i + 1)
    rep_far, token = replicas(place, far, held, "far")
    held = join(token, held, above, below, two_away)
    swapped = lax.ppermute(held, "c", SWAP)
    rep_both, _ = replicas(place, both, held, "both_first", (0, 1))
    halves = ((held, 0), (swapped, 0), (held, 1), (swapped, 1))
    prepared = [prepare(*half, 2 * index) for index, half in enumerate(halves)]
    weights, norms = [w for w, _ in prepared], [n for _, n in prepared]
    received = []
    for step, dx in enumerate(STEPS):
        if step == 3:
            norms[0], received[0] = tie(norms[0], received[0])
        if step == 1:
            rep_both, _ = replicas(place, both, beams, "both_rest", (1, 4))
        slots = (step, step, step, step - min(step, 1))
        beams = beams_block((rep_own, rep_near, rep_far, rep_both), slots, weights, norms, step)
        if dx:
            received.append(lax.ppermute(beams, "x", [(i, (i + dx) % 4) for i in range(4)]))
    return finish(place, received, beams, norms, float(NF * CH * 16))


def solution(mesh):
    fine = Mesh(mesh.devices.reshape(8, 2, 4, 2, 2), ("z", "yl", "x", "yh", "c"))
    return jax.shard_map(
        per_device,
        mesh=fine,
        in_specs=(
            P(None, None, ("z", "yl"), ("x", "yh", "c")),
            P(("z", "yl"), ("x", "yh", "c")),
            P(("x", "yh", "c")),
        ),
        out_specs=P(None, ("z", "yl", "x", "yh", "c")),
        check_vma=False,
    )
```

```python
import functools

import jax
import jax.numpy as jnp
import numpy as np
from jax import lax
from jax.experimental import pallas as pl
from jax.experimental.pallas import tpu as pltpu
from jax.sharding import Mesh, PartitionSpec as P

NFFT = 2048
lowest_bin = 37
bin_spacing = 29
f32 = jnp.float32
bf16 = jnp.bfloat16

NF = 8
ROWS = 256
CH = 256
COLS = 96
TILE = 32
NORM_ROWS = 8


SINE = [np.float32(1.570796305), np.float32(-0.6459629382), np.float32(0.07967590293), np.float32(-0.004592288967)]
COSINE = [np.float32(0.9999999724), np.float32(-1.233697014), np.float32(0.2535986436), np.float32(-0.02040835128)]


def horner(coefficients, value):
    total = coefficients[-1]
    for coefficient in coefficients[-2::-1]:
        total = coefficient + value * total
    return total


def unit_circle(turns_times, multiple):
    turns = turns_times * np.float32(multiple / NFFT)
    magic = np.float32(1.5 * 2**23)
    part = turns - ((turns + magic) - magic)
    square = part * part
    sine = part * horner(SINE, square)
    cosine = horner(COSINE, square)
    for _ in range(2):
        twice = sine + sine
        sine, cosine = twice * cosine, np.float32(1.0) - twice * sine
    return cosine, sine


def replica_tiles(tau):
    delay = tau.astype(f32)
    c0, s0 = unit_circle(delay, lowest_bin)
    cd, sd = unit_circle(delay, bin_spacing)
    cosines = [c0, c0 * cd - s0 * sd]
    sines = [s0, s0 * cd + c0 * sd]
    twice = cd + cd
    for _ in range(2, NF):
        cosines.append(twice * cosines[-1] - cosines[-2])
        sines.append(twice * sines[-1] - sines[-2])
    return cosines, sines


VMEM = pl.BlockSpec(memory_space=pltpu.VMEM)
BY_COLUMNS = (((1,), (1,)), ((), ()))


def product(left, right):
    return lax.dot_general(left, right, BY_COLUMNS, preferred_element_type=f32)


def eight_bits(values):
    scaled = values * np.float32(65537.0)
    return scaled - (scaled - values)


def thirds(values):
    high = eight_bits(values)
    rest = values - high
    middle = eight_bits(rest)
    return high.astype(bf16), middle.astype(bf16), (rest - middle).astype(bf16)


def exact_product(ones, values):
    high, middle, low = thirds(values)
    return product(ones, high) + (product(ones, middle) + product(ones, low))


def replicas_kernel(place, travel_ref, after_ref, rep_ref, token_ref):
    block = pl.program_id(0)
    token_ref[...] = jnp.zeros_like(token_ref)

    def body(step, carry):
        rows = pl.ds(pl.multiple_of(step * TILE, TILE), TILE)
        for half in range(CH // 128):
            lanes = slice(half * 128, (half + 1) * 128)
            cosines, sines = replica_tiles(travel_ref[0, rows, lanes].astype(jnp.int32))
            for f in range(NF):
                rep_ref[block, f, rows, lanes] = cosines[f].astype(bf16)
                rep_ref[block, f, rows, CH + half * 128 : CH + (half + 1) * 128] = sines[f].astype(bf16)
        return carry

    lax.fori_loop(0, ROWS // TILE, body, 0)


def replicas(place, travel, after, name, slots=(0, 4)):
    first, stop = slots

    def index(i, p):
        return (p[first + i], 0, 0)

    return pl.pallas_call(
        replicas_kernel,
        grid_spec=pltpu.PrefetchScalarGridSpec(
            num_scalar_prefetch=1,
            grid=(stop - first,),
            in_specs=[pl.BlockSpec((1, ROWS, CH), index), VMEM],
            out_specs=[VMEM, VMEM],
        ),
        out_shape=[
            jax.ShapeDtypeStruct((stop - first, NF, ROWS, 2 * CH), bf16),
            jax.ShapeDtypeStruct((8, 128), jnp.int32),
        ],
        cost_estimate=pl.CostEstimate(flops=40_000_000_000, bytes_accessed=1_000_000, transcendentals=0),
        compiler_params=pltpu.CompilerParams(vmem_limit_bytes=4 << 20),
        name=f"replicas_{name}",
    )(place, travel, after)


def join_kernel(*refs):
    *sources, token_ref, out_ref = refs
    rows = sources[0].shape[0]
    for index, source in enumerate(sources):
        out_ref[index * rows : (index + 1) * rows] = source[...]


def join(token, *arrays):
    first = arrays[0]
    return pl.pallas_call(
        join_kernel,
        in_specs=[VMEM] * (len(arrays) + 1),
        out_specs=VMEM,
        out_shape=jax.ShapeDtypeStruct((len(arrays) * first.shape[0],) + first.shape[1:], first.dtype),
        cost_estimate=pl.CostEstimate(flops=0, bytes_accessed=100_000, transcendentals=0),
        compiler_params=pltpu.CompilerParams(vmem_limit_bytes=2 << 20),
        name=f"join_{first.shape[0]}",
    )(*arrays, token)


def beams_kernel(*refs, slots):
    reps, weights, norms, out_ref = refs[0:4], refs[4:8], refs[8:12], refs[12]
    columns = []
    for f in range(NF):
        parts = [product(rep[slot, f], w_ref[f]) for rep, slot, w_ref in zip(reps, slots, weights)]
        columns.append((parts[0] + parts[1]) + (parts[2] + parts[3]))
    out_ref[0:ROWS] = jnp.concatenate(columns, axis=1).astype(out_ref.dtype)
    if out_ref.shape[0] > ROWS:
        out_ref[ROWS : ROWS + NORM_ROWS] = (norms[0][...] + norms[1][...]) + (norms[2][...] + norms[3][...])


def beams_block(reps, slots, weights, norms, step):
    own = STEPS[step] == 0
    rows = ROWS if own else ROWS + NORM_ROWS
    return pl.pallas_call(
        functools.partial(beams_kernel, slots=slots),
        in_specs=[VMEM] * 12,
        out_specs=VMEM,
        out_shape=jax.ShapeDtypeStruct((rows, NF * COLS), f32 if own else bf16),
        cost_estimate=pl.CostEstimate(flops=3_000_000_000, bytes_accessed=1_000_000, transcendentals=0),
        compiler_params=pltpu.CompilerParams(vmem_limit_bytes=4 << 20),
        name=f"beams_{step}",
    )(*reps, *weights, *norms)


def prepare_kernel(source_ref, w_ref, norm_ref, wide, *, flip, first_row):
    for g in range(16):
        class_row = 8 * (g // 4)
        for half in range(CH // 128):
            lanes = slice(half * 128, (half + 1) * 128)
            wide[half, g * 48 : (g + 1) * 48, :] = source_ref[class_row + 2 * (g % 4) + flip, :, lanes].astype(f32)
    squares = jnp.zeros((COLS, CH), f32)
    for f in range(NF):
        real, imag = [
            jnp.concatenate(
                [
                    jnp.concatenate(
                        [
                            wide[half, pl.ds(p * 24 + f * 3 + i, 16, stride=48), :]
                            for half in range(CH // 128)
                        ],
                        axis=1,
                    )
                    for i in range(3)
                ],
                axis=0,
            )
            for p in range(2)
        ]
        both = jnp.concatenate([real, imag], axis=0)
        squares = squares + both * both
        w_ref[f, :, 0:CH] = both.astype(bf16)
        w_ref[f, :, CH : 2 * CH] = jnp.concatenate([-imag, real], axis=0).astype(bf16)
    sums = exact_product(jnp.ones((NORM_ROWS, CH), bf16), squares)
    row = lax.broadcasted_iota(jnp.int32, sums.shape, 0) - first_row
    zero = jnp.zeros_like(sums)
    split = zero
    for index, part in enumerate(thirds(sums)[:2]):
        split = jnp.where(row == index, part.astype(f32), split)
    norm_ref[...] = jnp.concatenate([split] + [zero] * (NF - 1), axis=1).astype(bf16)


def prepare(source, flip, first_row):
    return pl.pallas_call(
        functools.partial(prepare_kernel, flip=flip, first_row=first_row),
        in_specs=[VMEM],
        out_specs=[VMEM, VMEM],
        scratch_shapes=[pltpu.VMEM((CH // 128, 768, 128), f32)],
        out_shape=[
            jax.ShapeDtypeStruct((NF, COLS, 2 * CH), bf16),
            jax.ShapeDtypeStruct((NORM_ROWS, NF * COLS), bf16),
        ],
        cost_estimate=pl.CostEstimate(flops=1_000_000_000, bytes_accessed=1_000_000, transcendentals=0),
        compiler_params=pltpu.CompilerParams(vmem_limit_bytes=6 << 20),
        name=f"prepare_{first_row}",
    )(source)


def column_tables():
    slot = np.arange(NF * COLS) % 48
    source = slot % 16
    step_z = np.array([0, 1, 7, 2])[source // 4]
    return np.stack([step_z, source % 2, source % 4 // 2 * 4, slot // 16]).astype(np.int32)


def finish_kernel(place, *refs, count):
    received, own_ref, norms, table_ref, out_ref = refs[0:3], refs[3], refs[4:8], refs[8], refs[9]
    window = lax.broadcasted_iota(jnp.int32, (48, NF * COLS), 0)
    step_z, flip_yl, flip_z, part = [table_ref[row : row + 1, :] for row in range(4)]
    z, yl = place[4], place[5]
    step_z = step_z + jnp.where(step_z == 2, 4 * (1 - z % 2), 0)
    source = 2 * (((z + step_z) & 7) ^ flip_z) + (yl ^ flip_yl)
    pick = jnp.where(window == 3 * source + part, 1.0, 0.0).astype(bf16)
    beams = own_ref[...]
    norm_rows = sum(ref[...].astype(f32) for ref in norms)
    for ref in received:
        beams = beams + ref[0:ROWS].astype(f32)
        norm_rows = norm_rows + ref[ROWS : ROWS + NORM_ROWS].astype(f32)
    norm_sum = jnp.sum(exact_product(pick, norm_rows), axis=1, keepdims=True)
    window_norm = norm_sum / count + 1e-06
    out_ref[...] = exact_product(pick, beams * beams) / (count * window_norm)


def finish(place, received, own, norms, count):
    return pl.pallas_call(
        functools.partial(finish_kernel, count=count),
        in_specs=[pl.BlockSpec(memory_space=pltpu.SMEM)] + [VMEM] * 9,
        out_specs=VMEM,
        out_shape=jax.ShapeDtypeStruct((48, ROWS), f32),
        compiler_params=pltpu.CompilerParams(vmem_limit_bytes=8 << 20),
        name="finish",
    )(place, *received, own, *norms, jnp.asarray(column_tables()))


STEPS = (2, 1, 3, 0)
SWAP = [(0, 1), (1, 0)]


def tie(*values):
    return lax.optimization_barrier(values)


def per_device(spectra, travel, quality):
    x, yh, core = lax.axis_index("x"), lax.axis_index("yh"), lax.axis_index("c")
    order = [(x + dx) % 4 for dx in STEPS]
    place = jnp.stack(order + [lax.axis_index("z"), lax.axis_index("yl")]).astype(jnp.int32)
    blocks = travel.reshape(4, 2, 2, ROWS, CH)

    def travel_for(flip_y, flip_c):
        return lax.dynamic_slice(
            blocks, (0, yh ^ flip_y, core ^ flip_c, 0, 0), (4, 1, 1, ROWS, CH)
        ).reshape(4, ROWS, CH).astype(jnp.int16)

    block = (spectra * quality.astype(bf16)).reshape(1, 48, CH)
    parts = [travel_for(flip // 2, flip % 2) for flip in range(4)]
    place, *parts = tie(place, *parts)

    def moved(flip):
        return lax.ppermute(parts[flip], ("yh", "c"), [(i, i ^ flip) for i in range(4)])

    def along_z(values, target):
        return lax.ppermute(values, "z", [(i, target(i) % 8) for i in range(8)])

    held = block
    other = lax.ppermute(held, "yh", SWAP)
    held = join(other, held, other)
    held, *parts = tie(held, *parts)
    far, both = moved(2), moved(3)
    other = lax.ppermute(held, "yl", SWAP)
    held = join(other, held, other)
    held, parts[1] = tie(held, parts[1])
    near = moved(1)
    other = along_z(held, lambda i: i ^ 4)
    rep_own, token = replicas(place, parts[0], held, "own")
    rep_near, token = replicas(place, near, token, "near")
    held = join(token, held, other)
    two_away = along_z(held, lambda i: i - 2 if i % 2 else i + 2)
    above = along_z(held, lambda i: i - 1)
    below = along_z(held, lambda i: i + 1)
    rep_far, token = replicas(place, far, held, "far")
    held = join(token, held, above, below, two_away)
    swapped = lax.ppermute(held, "c", SWAP)
    rep_both, _ = replicas(place, both, held, "both_first", (0, 1))
    halves = ((held, 0), (swapped, 0), (held, 1), (swapped, 1))
    prepared = [prepare(*half, 2 * index) for index, half in enumerate(halves)]
    weights, norms = [w for w, _ in prepared], [n for _, n in prepared]
    received = []
    for step, dx in enumerate(STEPS):
        if step == 3:
            norms[0], received[0] = tie(norms[0], received[0])
        if step == 1:
            rep_both, _ = replicas(place, both, beams, "both_rest", (1, 4))
        slots = (step, step, step, step - min(step, 1))
        beams = beams_block((rep_own, rep_near, rep_far, rep_both), slots, weights, norms, step)
        if dx:
            received.append(lax.ppermute(beams, "x", [(i, (i + dx) % 4) for i in range(4)]))
    return finish(place, received, beams, norms, float(NF * CH * 16))


def solution(mesh):
    fine = Mesh(mesh.devices.reshape(8, 2, 4, 2, 2), ("z", "yl", "x", "yh", "c"))
    return jax.shard_map(
        per_device,
        mesh=fine,
        in_specs=(
            P(None, None, ("z", "yl"), ("x", "yh", "c")),
            P(("z", "yl"), ("x", "yh", "c")),
            P(("x", "yh", "c")),
        ),
        out_specs=P(None, ("z", "yl", "x", "yh", "c")),
        check_vma=False,
    )
```
